32 devices in a mesh: dir: 8 (over y, x, core), freq: 4 (over z).
Axes of the slice: x: 2, y: 2, z: 4, core: 2. Of those that a mesh axis runs over, the one named last changes fastest.
Arguments:
- observed: float32 [512, 8, 2, 2, 512], P('dir', 'freq'), as said below
- flags: int32 [512, 2, 512], P('dir'), may hold values from 0 to 1, as said below
- screen: float32 [16, 512], P('dir'), may hold values from -6 to 6
- screen_kernel: float32 [512, 512], replicated
- station_uv: float32 [2, 2, 512], replicated, may hold values from -360 to 360
- source_lm: float32 [2, 3072], P(None, 'dir'), may hold values from -0.05 to 0.05
- source_flux: float32 [3072], P('dir')
- station_gain: bfloat16 [8, 2, 2, 512, 3072], P('freq', None, None, None, 'dir'), may hold values from -4.1875 to 4.1875
- source_direction: int32 [3072], P('dir'), may hold values from 0 to 1
- freq_ratio: float32 [8], P('freq')
Outputs:
- residual: float32 [512, 8, 2, 2, 512], P('dir', 'freq')
- updated_screen: float32 [16, 512], P('dir')
The draws below stay inside these ranges and needn't reach their ends.
Inputs may be any that keep to these rules, and one draw needn't show every extreme that they name: observed is Hermitian in its stations: observed[p, f, t, 0, q] equals observed[q, f, t, 0, p] and observed[p, f, t, 1, q] equals minus observed[q, f, t, 1, p]. flags[p, t, q] equals flags[q, t, p].
All inputs are finite; a program needn't handle non-finite values.
Results may differ from the reference program's by a relative error of at most 0.0037.
Values may be sent and summed in bfloat16 or wider, within the bound.
A program may use at most 128 MiB of HBM per device.

```python
import math
import jax
import jax.numpy as jnp
from jax import lax

S = 512
DIR_DEV = 2
SRC_DEV = 384
TIMES = 2
DIRS = 16
SOURCES = 3072
FREQS = 8


def draw_observed(key, part):
    key_real, key_imag = jax.random.split(key, 2)
    first = jax.random.normal(key_real, (FREQS, TIMES, S, S), jnp.float32)
    second = jax.random.normal(key_imag, (FREQS, TIMES, S, S), jnp.float32)
    real_part = (first + jnp.swapaxes(first, 2, 3)) * 0.7071
    imag_part = (second - jnp.swapaxes(second, 2, 3)) * 0.7071
    stacked = jnp.stack([real_part, imag_part], axis=2)
    return jnp.transpose(stacked, (3, 0, 1, 2, 4))


def draw_flags(key, part):
    levels = jax.random.randint(key, (TIMES, S, S), 0, 10)
    kept = (levels >= 1).astype(jnp.int32)
    station_ids = jnp.arange(S, dtype=jnp.int32)
    upper = station_ids[:, None] < station_ids[None, :]
    symmetric = jnp.where(upper[None], kept, jnp.swapaxes(kept, 1, 2))
    return jnp.transpose(symmetric, (1, 0, 2))


def draw_screen_kernel(key, part):
    factor = jax.random.normal(key, (S, S), jnp.float32)
    product = jnp.dot(factor, factor.T, precision=lax.Precision.HIGHEST) / S
    return product + 0.5 * jnp.eye(S, dtype=jnp.float32)


def draw_source_flux(key, part):
    position = jnp.arange(SOURCES, dtype=jnp.float32) / (SOURCES - 1)
    slope = 1.0 + 2.0 * position
    base = jnp.exp(jax.random.uniform(key, (SOURCES,), jnp.float32, minval=math.log(0.3), maxval=0.0))
    return base * slope


def draw_freq_ratio(key, part):
    offset = jax.random.uniform(key, (FREQS,), jnp.float32)
    return 0.5 * 3.0 ** ((jnp.arange(FREQS, dtype=jnp.float32) + offset) / FREQS)


def set_ends(drawn, own_key, low, top_value):
    extent = drawn.shape
    place = [jax.random.randint(jax.random.fold_in(own_key, axis), (), 0, extent[axis]) for axis in range(len(extent))]
    drawn = drawn.at[tuple(place)].set(low)
    longest = extent.index(max(extent))
    place[longest] = (place[longest] + 1) % extent[longest]
    return drawn.at[tuple(place)].set(top_value)


def shard_levels(stream_key, extent, cuts, least, top_value):
    factor_of, own = 1.0, jax.random.fold_in(stream_key, 6)
    for dim, shards_of in cuts:
        steps = jnp.exp(jax.random.uniform(jax.random.fold_in(own, dim), (shards_of,), jnp.float32, least / len(cuts), top_value / len(cuts)))
        factor_of = factor_of * jnp.repeat(steps, extent[dim] // shards_of).reshape([-1 if axis == dim else 1 for axis in range(len(extent))])
    return factor_of


def scatter_about(stream_key, dims, deviation, reach, cuts=(), kind=jnp.bfloat16):
    drawn = deviation * jax.random.normal(stream_key, dims, jnp.float32)
    if cuts:
        drawn = drawn * shard_levels(stream_key, dims, cuts, -0.22, 0.18)
    return jnp.clip(drawn, -reach, reach).astype(kind)


def setup_inputs(seed: int = 0) -> dict:
    splits = jax.random.split(jax.random.key(seed), 11)
    observed = draw_observed(jax.random.fold_in(splits[10], 71), 0)
    flags = draw_flags(jax.random.fold_in(splits[10], 71), 0)
    screen = scatter_about(splits[2], (DIRS, S), 1.0, 6.0, ((0, 8),), jnp.float32)
    screen_kernel = draw_screen_kernel(jax.random.fold_in(splits[10], 71), 0)
    station_uv = scatter_about(splits[4], (TIMES, 2, S), 60.0, 360.0, (), jnp.float32)
    source_lm = jnp.clip(jax.random.uniform(splits[5], (2, SOURCES), jnp.float32, -0.05, 0.05) * shard_levels(splits[5], (2, SOURCES), ((1, 8),), -0.4, 0.0), -0.05, 0.05)
    source_flux = draw_source_flux(jax.random.fold_in(splits[10], 71), 0)
    station_gain = scatter_about(splits[7], (FREQS, TIMES, 2, S, SOURCES), 0.7, 4.1875, ((0, 4), (4, 8)))
    source_direction = set_ends(jax.random.randint(splits[8], (SOURCES,), 0, DIR_DEV), jax.random.fold_in(splits[8], 1), 0, DIR_DEV - 1).astype(jnp.int32)
    freq_ratio = draw_freq_ratio(jax.random.fold_in(splits[10], 71), 0)
    return dict(observed=observed, flags=flags, screen=screen, screen_kernel=screen_kernel, station_uv=station_uv, source_lm=source_lm, source_flux=source_flux, station_gain=station_gain, source_direction=source_direction, freq_ratio=freq_ratio)


step_size = 0.3
epsilon = 1e-06
highest = lax.Precision.HIGHEST

def reference(observed, flags, screen, screen_kernel, station_uv, source_lm, source_flux, station_gain, source_direction, freq_ratio):
    sources = source_flux.shape[0]
    scaling = 1.0 / math.sqrt(sources)
    owner_dir = jnp.arange(sources, dtype=jnp.int32) // SRC_DEV * DIR_DEV + source_direction
    onehot_dirs = (owner_dir[:, None] == jnp.arange(DIRS, dtype=jnp.int32)[None, :]).astype(jnp.float32)
    screen_src = jnp.dot(onehot_dirs, screen, precision=highest).T
    amplitude = jnp.sqrt(source_flux)
    station_ids = jnp.arange(S, dtype=jnp.int32)
    cross_baseline = (station_ids[:, None] != station_ids[None, :]).astype(jnp.float32)

    def per_matrix(matrix_index):
        channel = matrix_index // TIMES
        moment = matrix_index % TIMES
        frequency = freq_ratio[channel]
        uv_now = station_uv[moment]
        gain_now = station_gain[channel, moment].astype(jnp.float32)
        geometry = uv_now[0][:, None] * source_lm[0][None, :] + uv_now[1][:, None] * source_lm[1][None, :]
        phase_angle = screen_src / frequency + 2.0 * math.pi * frequency * geometry
        cosine = jnp.cos(phase_angle)
        sine = jnp.sin(phase_angle)
        phasor_re = (amplitude[None, :] * (gain_now[0] * cosine - gain_now[1] * sine)).astype(jnp.bfloat16)
        phasor_im = (amplitude[None, :] * (gain_now[0] * sine + gain_now[1] * cosine)).astype(jnp.bfloat16)
        left_mat = jnp.concatenate([phasor_re, phasor_im], axis=1)
        skew_mat = jnp.concatenate([phasor_im, -phasor_re], axis=1)
        real_part = jnp.dot(left_mat, left_mat.T, preferred_element_type=jnp.float32) * scaling
        imag_part = jnp.dot(skew_mat, left_mat.T, preferred_element_type=jnp.float32) * scaling
        model = jnp.stack([real_part, imag_part], axis=1)
        baseline_keep = flags[:, moment, :].astype(jnp.float32) * cross_baseline
        residual = baseline_keep[:, None, :] * (observed[:, channel, moment] - model)
        resid_half = residual.astype(jnp.bfloat16)
        row_prod = jnp.dot(resid_half[:, 0], left_mat, preferred_element_type=jnp.float32)
        row_prod = row_prod + jnp.dot(resid_half[:, 1], -skew_mat, preferred_element_type=jnp.float32)
        conj_mat = jnp.concatenate([phasor_re, -phasor_im], axis=1)
        dual_mat = jnp.concatenate([phasor_im, phasor_re], axis=1)
        col_prod = jnp.dot(resid_half[:, 0].T, conj_mat, preferred_element_type=jnp.float32)
        col_prod = col_prod + jnp.dot(resid_half[:, 1].T, dual_mat, preferred_element_type=jnp.float32)
        weight_re = row_prod[:, :sources] + col_prod[:, :sources]
        weight_im = row_prod[:, sources:] - col_prod[:, sources:]
        source_grad = phasor_im.astype(jnp.float32) * weight_re - phasor_re.astype(jnp.float32) * weight_im
        grad_now = jnp.dot(source_grad, onehot_dirs, precision=highest).T * (scaling / frequency)
        return (residual, grad_now)
    residuals, grads = lax.map(per_matrix, jnp.arange(FREQS * TIMES, dtype=jnp.int32))
    residual_all = jnp.transpose(residuals.reshape(FREQS, TIMES, S, 2, S), (2, 0, 1, 3, 4))
    gradient = lax.optimization_barrier(jnp.sum(grads, axis=0))
    smooth = jnp.dot(gradient, screen_kernel, precision=highest)
    mean_sq = jnp.mean(smooth * smooth)
    updated = screen - step_size * smooth / jnp.sqrt(mean_sq + epsilon)
    return (residual_all, updated)
```

```python
import functools
import math

import jax
import jax.numpy as jnp
from jax import lax
from jax.experimental import pallas as pl
from jax.experimental.pallas import tpu as pltpu
from jax.sharding import PartitionSpec as P

step_size = 0.3
epsilon = 1e-06
MESH = pl.DeviceIdType.MESH
f32 = jnp.float32
bf16 = jnp.bfloat16

SIN_POLY = (6.283185272722381, -41.341697068949564, 81.60502462236155, -76.70155117323625, 42.01616580115987, -14.868610927638132, 3.19969357384433)
COS_POLY = (0.9999999891722522, -19.739204532086525, 64.93911898351571, -85.45016554378464, 60.16783168053616, -25.968313120273056, 6.5296101719799085)


def horner(coefs, z):
    total = jnp.full_like(z, coefs[-1])
    for c in coefs[-2::-1]:
        total = total * z + c
    return total


def kernel(
    n_dir,
    n_freq,
    scaling,
    ratio_ref,
    gain_hbm,
    cols_ref,
    src_ref,
    dirs_ref,
    kobs_hbm,
    keep_hbm,
    screen_ref,
    kern_hbm,
    own_ref,
    mirror_ref,
    updated_ref,
    gain,
    kobs,
    keep,
    kern,
    left,
    mixed,
    pfull,
    pdir,
    s1buf,
    r1buf,
    s2buf,
    qown,
    r2buf,
    ugath,
    rowacc,
    colacc,
    gbuf,
    sqbuf,
    tbuf,
    gain_sem,
    in_sem,
    s1_send,
    s1_recv,
    s2_send,
    s2_recv,
    ag_send,
    ag_recv,
    fw_send,
    fr_send,
    fr_recv,
    sq_send,
    sq_recv,
):
    count, _, stations, sources = gain.shape
    local_dirs = pdir.shape[0]
    times = keep.shape[0]
    rows = kobs.shape[1]
    chips = n_dir // 2
    me = lax.axis_index("dir")
    fme = lax.axis_index("freq")
    core = lax.rem(me, 2)
    chip = lax.div(me, 2)
    partner = chip * 2 + 1 - core

    def gain_copy(m):
        return pltpu.make_async_copy(gain_hbm.at[m], gain.at[m], gain_sem.at[m])

    for m in range(count):
        gain_copy(m).start()
    in_copies = [
        pltpu.make_async_copy(kobs_hbm, kobs, in_sem.at[0]),
        pltpu.make_async_copy(keep_hbm, keep, in_sem.at[1]),
        pltpu.make_async_copy(kern_hbm, kern, in_sem.at[2]),
    ]
    for c in in_copies:
        c.start()

    barrier = pltpu.get_barrier_semaphore()
    for o in range(1, n_dir):
        pl.semaphore_signal(
            barrier, inc=1, device_id={"dir": lax.rem(me + o, n_dir)}, device_id_type=MESH
        )
    for o in range(1, n_freq):
        pl.semaphore_signal(
            barrier, inc=1, device_id={"freq": lax.rem(fme + o, n_freq)}, device_id_type=MESH
        )

    rowacc[...] = jnp.zeros_like(rowacc)
    colacc[...] = jnp.zeros_like(colacc)

    def remote(src, dst, send, recv, axis, where):
        return pltpu.make_async_remote_copy(
            src_ref=src,
            dst_ref=dst,
            send_sem=send,
            recv_sem=recv,
            device_id={axis: where},
            device_id_type=MESH,
        )

    def s1_copy(m):
        return remote(s1buf.at[m], r1buf.at[m], s1_send.at[m], s1_recv.at[m], "dir", partner)

    def s2_copy(m, o):
        to = lax.rem(chip + o, chips)
        return remote(
            s2buf.at[m, to],
            r2buf.at[m, o],
            s2_send.at[m, o],
            s2_recv.at[m, o],
            "dir",
            to * 2 + core,
        )

    def row_slice(owner):
        return pl.ds(pl.multiple_of(owner * rows, rows), rows)

    def ag_copy(m, o):
        to = partner if o == 0 else lax.rem(chip + o, chips) * 2 + core
        piece = ugath.at[m, row_slice(me), :]
        return remote(piece, piece, ag_send.at[m, o], ag_recv.at[m, o], "dir", to)

    def fw_copy(m, o):
        owner = lax.rem(chip - o + chips, chips) * 2 + core
        piece = ugath.at[m, row_slice(owner), :]
        return remote(piece, piece, fw_send.at[m, o], ag_recv.at[m, chips + o - 1], "dir", partner)

    chunk = 32

    def phasors(m):
        gain_copy(m).wait()

        def one(i, _):
            at = pl.ds(pl.multiple_of(i * chunk, chunk), chunk)
            col = cols_ref[m, at, :]
            lm = src_ref[...]
            turns = col[:, 0:1] * lm[0:1] + col[:, 1:2] * lm[1:2]
            own = jnp.broadcast_to(col[:, 2:3], turns.shape)
            for d in range(1, local_dirs):
                own = jnp.where(dirs_ref[0:1, :] == d, col[:, 2 + d : 3 + d], own)
            turns = turns + own
            r = turns - jnp.round(turns)
            z = r * r
            amp = lm[2:3]
            sine = horner(SIN_POLY, z) * (r * amp)
            cosine = horner(COS_POLY, z) * amp
            g_re = gain[m, 0, at, :].astype(f32)
            g_im = gain[m, 1, at, :].astype(f32)
            re = (g_re * cosine - g_im * sine).astype(bf16)
            im = (g_re * sine + g_im * cosine).astype(bf16)
            left[m, at, :sources] = re
            left[m, at, sources:] = im
            re = re.astype(f32)
            im = im.astype(f32)
            mixed[m, at, :sources] = (re + im).astype(bf16)
            mixed[m, at, sources:] = (im - re).astype(bf16)
            return 0

        lax.fori_loop(0, stations // chunk, one, 0)

    def nt_dot(a, b):
        return lax.dot_general(a, b, (((1,), (1,)), ((), ())), preferred_element_type=f32)

    def partial_model(m):
        pfull[m] = nt_dot(mixed[m], left[m]).reshape(chips, 2, rows, stations)

        def one(j, _):
            s1buf[m, j] = pfull[m, j, 1 - core].astype(bf16)
            return 0

        lax.fori_loop(0, chips, one, 0)

    def chip_sum(m):
        s1_copy(m).wait_recv()

        def one(j, _):
            total = pfull[m, j, core] + r1buf[m, j].astype(f32)
            s2buf[m, j] = total.astype(bf16)
            return 0

        lax.fori_loop(0, chips, one, 0)
        for o in range(1, chips):
            s2_copy(m, o).start()
        qown[m] = pfull[m, chip, core] + r1buf[m, chip].astype(f32)

    def own_residual(m):
        total = qown[m]
        for o in range(1, chips):
            s2_copy(m, o).wait_recv()
            total = total + r2buf[m, o].astype(f32)
        value = kobs[m] - keep[lax.rem(m, times)] * (total * scaling)
        own_ref[m] = value
        ugath[m, row_slice(me), :] = value.astype(bf16)
        for o in list(range(1, chips)) + [0]:
            ag_copy(m, o).start()

    def forward(m):
        for o in range(1, chips):
            ag_copy(m, o).wait_recv()
            fw_copy(m, o).start()

    def direction_models(m):
        for d in range(local_dirs):
            mask = jnp.where(dirs_ref[...] == d, 1.0, 0.0).astype(bf16)
            mask = jnp.concatenate([mask, mask], axis=1)[0:1]
            pdir[d] = nt_dot(left[m] * mask, mixed[m])

    def local_grad(m):
        ag_copy(m, 0).wait_recv()
        for o in range(1, chips):
            fw_copy(m, o).wait_recv()
        weight = scaling / ratio_ref[0, lax.div(m, times)]

        def one(i, carry):
            at = pl.ds(pl.multiple_of(i * chunk, chunk), chunk)
            u = ugath[m, at, :].astype(f32) * weight
            out = []
            for d in range(local_dirs):
                w = u * pdir[d, at, :]
                part = w[:, 0:128]
                for b in range(1, stations // 128):
                    part = part + w[:, b * 128 : (b + 1) * 128]
                rowacc[d, at, :] += part
                c = carry[d]
                for b in range(chunk // 8):
                    c = c + w[b * 8 : (b + 1) * 8]
                out.append(c)
            return tuple(out)

        init = tuple(colacc[d] for d in range(local_dirs))
        out = lax.fori_loop(0, stations // chunk, one, init)
        for d in range(local_dirs):
            colacc[d] = out[d]

    def step(s, _):
        @pl.when(s < count)
        def _():
            phasors(s)
            partial_model(s)

            @pl.when(s == 0)
            def _():
                pl.semaphore_wait(barrier, n_dir - 1 + n_freq - 1)
                for c in in_copies:
                    c.wait()

            s1_copy(s).start()

        @pl.when(jnp.logical_and(s >= 1, s < count + 1))
        def _():
            chip_sum(s - 1)

        @pl.when(jnp.logical_and(s >= 2, s < count + 2))
        def _():
            own_residual(s - 2)

        @pl.when(jnp.logical_and(s >= 3, s < count + 3))
        def _():
            forward(s - 3)

        @pl.when(s >= 4)
        def _():
            local_grad(s - 4)

        @pl.when(jnp.logical_and(s >= 3, s < count + 3))
        def _():
            direction_models(s - 3)

        return 0

    lax.fori_loop(0, count + 4, step, 0)

    mine = []
    for d in range(local_dirs):
        by_col = jnp.sum(colacc[d], axis=0, keepdims=True)
        by_row = jnp.sum(jnp.transpose(rowacc[d]), axis=0, keepdims=True)
        mine.append(by_col - by_row)
    mine.append(jnp.zeros((8 - local_dirs, stations), f32))
    gbuf[fme] = jnp.concatenate(mine, axis=0)

    def fr_copy(o):
        slot = gbuf.at[fme]
        return remote(
            slot, slot, fr_send.at[o], fr_recv.at[o], "freq", lax.rem(fme + o, n_freq)
        )

    for o in range(1, n_freq):
        fr_copy(o).start()

    group = 128 // rows
    lane0 = pl.multiple_of(lax.div(me, group) * 128, 128)
    sub0 = pl.multiple_of(lax.rem(me, group) * rows, rows)

    def mirror(m, _):
        for b in range(stations // 128):
            block = ugath[m, b * 128 : (b + 1) * 128, pl.ds(lane0, 128)].astype(f32)
            tbuf[:, b * 128 : (b + 1) * 128] = jnp.transpose(block)
        mirror_ref[m] = tbuf[pl.ds(sub0, rows), :]
        return 0

    lax.fori_loop(0, count, mirror, 0)

    for o in range(1, n_freq):
        fr_copy(o).wait_recv()
    total = gbuf[0]
    for f in range(1, n_freq):
        total = total + gbuf[f]
    smooth = jnp.dot(
        total, kern[...], preferred_element_type=f32, precision=lax.Precision.HIGHEST
    )
    squares = smooth * smooth
    part = squares[:, 0:128]
    for b in range(1, stations // 128):
        part = part + squares[:, b * 128 : (b + 1) * 128]
    sqbuf[0] = part

    def sq_copy(o):
        return remote(
            sqbuf.at[0], sqbuf.at[o], sq_send.at[o], sq_recv.at[o], "dir", lax.rem(me + o, n_dir)
        )

    for o in range(1, n_dir):
        sq_copy(o).start()
    for o in range(1, n_dir):
        sq_copy(o).wait_recv()
        part = part + sqbuf[o]
    total_sq = jnp.sum(jnp.sum(part, axis=1, keepdims=True), axis=0, keepdims=True)
    scale = step_size * lax.rsqrt(total_sq / (local_dirs * n_dir * stations) + epsilon)
    updated_ref[...] = screen_ref[...] - smooth[:local_dirs] * scale

    def drain(m, _):
        s1_copy(m).wait_send()
        for o in range(1, chips):
            s2_copy(m, o).wait_send()
            fw_copy(m, o).wait_send()
        for o in range(chips):
            ag_copy(m, o).wait_send()
        return 0

    lax.fori_loop(0, count, drain, 0)
    for o in range(1, n_freq):
        fr_copy(o).wait_send()
    for o in range(1, n_dir):
        sq_copy(o).wait_send()


def body(
    observed,
    flags,
    screen,
    screen_kernel,
    station_uv,
    source_lm,
    source_flux,
    station_gain,
    source_direction,
    freq_ratio,
):
    n_dir = lax.axis_size("dir")
    n_freq = lax.axis_size("freq")
    local_dirs, stations = screen.shape
    sources = source_flux.shape[0]
    rows = observed.shape[0]
    channels = freq_ratio.shape[0]
    times = station_uv.shape[0]
    count = channels * times
    chips = n_dir // 2
    scaling = 1.0 / math.sqrt(sources * n_dir)

    gain = station_gain.reshape(count, 2, stations, sources)
    freq_each = jnp.repeat(freq_ratio, times)
    uv = jnp.tile(station_uv, (channels, 1, 1)) * freq_each[:, None, None]
    screens = screen[None] / (freq_each * (2.0 * math.pi))[:, None, None]
    cols = jnp.concatenate([uv, screens], axis=1)
    cols = jnp.pad(cols, ((0, 0), (0, 8 - cols.shape[1]), (0, 0)))
    cols = jnp.transpose(cols, (0, 2, 1))
    src = jnp.concatenate([source_lm, jnp.sqrt(source_flux)[None]], axis=0)
    src = jnp.pad(src, ((0, 8 - src.shape[0]), (0, 0)))
    dirs = jnp.broadcast_to(source_direction[None], (8, sources))

    row_ids = lax.axis_index("dir") * rows + jnp.arange(rows, dtype=jnp.int32)
    cross = row_ids[:, None] != jnp.arange(stations, dtype=jnp.int32)[None, :]
    keep = jnp.transpose(flags, (1, 0, 2)).astype(f32) * cross.astype(f32)[None]
    packed = (observed[:, :, :, 0] + observed[:, :, :, 1]).reshape(rows, count, stations)
    kobs = jnp.transpose(packed, (1, 0, 2)) * jnp.tile(keep, (channels, 1, 1))

    vmem = pl.BlockSpec(memory_space=pltpu.VMEM)
    hbm = pl.BlockSpec(memory_space=pl.ANY)
    dma = pltpu.SemaphoreType.DMA
    own, mirrored, updated = pl.pallas_call(
        functools.partial(kernel, n_dir, n_freq, scaling),
        out_shape=(
            jax.ShapeDtypeStruct((count, rows, stations), f32),
            jax.ShapeDtypeStruct((count, rows, stations), f32),
            jax.ShapeDtypeStruct((local_dirs, stations), f32),
        ),
        in_specs=[
            pl.BlockSpec(memory_space=pltpu.SMEM),
            hbm,
            vmem,
            vmem,
            vmem,
            hbm,
            hbm,
            vmem,
            hbm,
        ],
        out_specs=(vmem, vmem, vmem),
        scratch_shapes=[
            pltpu.VMEM((count, 2, stations, sources), bf16),
            pltpu.VMEM((count, rows, stations), f32),
            pltpu.VMEM((times, rows, stations), f32),
            pltpu.VMEM((stations, stations), f32),
            pltpu.VMEM((count, stations, 2 * sources), bf16),
            pltpu.VMEM((count, stations, 2 * sources), bf16),
            pltpu.VMEM((count, chips, 2, rows, stations), f32),
            pltpu.VMEM((local_dirs, stations, stations), f32),
            pltpu.VMEM((count, chips, rows, stations), bf16),
            pltpu.VMEM((count, chips, rows, stations), bf16),
            pltpu.VMEM((count, chips, rows, stations), bf16),
            pltpu.VMEM((count, rows, stations), f32),
            pltpu.VMEM((count, chips, rows, stations), bf16),
            pltpu.VMEM((count, stations, stations), bf16),
            pltpu.VMEM((local_dirs, stations, 128), f32),
            pltpu.VMEM((local_dirs, 8, stations), f32),
            pltpu.VMEM((n_freq, 8, stations), f32),
            pltpu.VMEM((n_dir, 8, 128), f32),
            pltpu.VMEM((128, stations), f32),
            dma((count,)),
            dma((3,)),
            dma((count,)),
            dma((count,)),
            dma((count, chips)),
            dma((count, chips)),
            dma((count, chips)),
            dma((count, 2 * chips)),
            dma((count, chips)),
            dma((n_freq,)),
            dma((n_freq,)),
            dma((n_dir,)),
            dma((n_dir,)),
        ],
        compiler_params=pltpu.CompilerParams(
            collective_id=0, has_side_effects=True, vmem_limit_bytes=60 * 1024 * 1024
        ),
        name="calibrate",
    )(
        freq_ratio[None],
        gain,
        cols,
        src,
        dirs,
        kobs,
        keep,
        screen,
        screen_kernel,
    )
    residual = jnp.stack([(own + mirrored) * 0.5, (own - mirrored) * 0.5], axis=1)
    residual = jnp.transpose(residual, (2, 0, 1, 3))
    return (residual.reshape(observed.shape), updated)


def solution(mesh):
    placed = (
        P("dir", "freq", None, None, None),
        P("dir", None, None),
        P("dir", None),
        P(),
        P(),
        P(None, "dir"),
        P("dir"),
        P("freq", None, None, None, "dir"),
        P("dir"),
        P("freq"),
    )
    return jax.shard_map(
        body,
        mesh=mesh,
        in_specs=placed,
        out_specs=(P("dir", "freq", None, None, None), P("dir", None)),
        check_vma=False,
    )
```

```python
import functools
import math

import jax
import jax.numpy as jnp
from jax import lax
from jax.experimental import pallas as pl
from jax.experimental.pallas import tpu as pltpu
from jax.sharding import PartitionSpec as P

step_size = 0.3
epsilon = 1e-06
MESH = pl.DeviceIdType.MESH
f32 = jnp.float32
bf16 = jnp.bfloat16

SIN_POLY = (6.283185272722381, -41.341697068949564, 81.60502462236155, -76.70155117323625, 42.01616580115987, -14.868610927638132, 3.19969357384433)
COS_POLY = (0.9999999891722522, -19.739204532086525, 64.93911898351571, -85.45016554378464, 60.16783168053616, -25.968313120273056, 6.5296101719799085)


def horner(coefs, z):
    total = jnp.full_like(z, coefs[-1])
    for c in coefs[-2::-1]:
        total = total * z + c
    return total


def kernel(
    n_dir,
    n_freq,
    scaling,
    ratio_ref,
    gain_hbm,
    uv_ref,
    lm_ref,
    flux_ref,
    dirs_ref,
    obs_hbm,
    flags_hbm,
    screen_ref,
    kern_hbm,
    resid_ref,
    updated_ref,
    gain,
    obs,
    flags,
    kern,
    cols,
    own_res,
    left,
    mixed,
    pfull,
    pdir,
    s1buf,
    r1buf,
    s2buf,
    qown,
    r2buf,
    ugath,
    rowacc,
    colacc,
    gbuf,
    sqbuf,
    tbuf,
    gain_sem,
    in_sem,
    s1_send,
    s1_recv,
    s2_send,
    s2_recv,
    ag_send,
    ag_recv,
    fw_send,
    fr_send,
    fr_recv,
    sq_send,
    sq_recv,
):
    count, _, stations, sources = gain.shape
    local_dirs = pdir.shape[0]
    times = uv_ref.shape[0]
    rows = own_res.shape[1]
    tiles = stations // 128
    chips = n_dir // 2
    me = lax.axis_index("dir")
    fme = lax.axis_index("freq")
    core = lax.rem(me, 2)
    chip = lax.div(me, 2)
    partner = chip * 2 + 1 - core

    def gain_copy(m):
        return pltpu.make_async_copy(gain_hbm.at[m], gain.at[m], gain_sem.at[m])

    for m in range(count):
        gain_copy(m).start()
    in_copies = [
        pltpu.make_async_copy(obs_hbm, obs, in_sem.at[0]),
        pltpu.make_async_copy(flags_hbm, flags, in_sem.at[1]),
        pltpu.make_async_copy(kern_hbm, kern, in_sem.at[2]),
    ]
    for c in in_copies:
        c.start()

    barrier = pltpu.get_barrier_semaphore()
    for o in range(1, n_dir):
        pl.semaphore_signal(
            barrier, inc=1, device_id={"dir": lax.rem(me + o, n_dir)}, device_id_type=MESH
        )
    for o in range(1, n_freq):
        pl.semaphore_signal(
            barrier, inc=1, device_id={"freq": lax.rem(fme + o, n_freq)}, device_id_type=MESH
        )

    for m in range(count):
        ratio = ratio_ref[0, m // times]
        parts = [uv_ref[m % times] * ratio, screen_ref[...] / (ratio * (2.0 * math.pi))]
        parts.append(jnp.zeros((8 - 2 - local_dirs, stations), f32))
        cols[m] = jnp.transpose(jnp.concatenate(parts, axis=0))
    rowacc[...] = jnp.zeros_like(rowacc)
    colacc[...] = jnp.zeros_like(colacc)

    def remote(src, dst, send, recv, axis, where):
        return pltpu.make_async_remote_copy(
            src_ref=src,
            dst_ref=dst,
            send_sem=send,
            recv_sem=recv,
            device_id={axis: where},
            device_id_type=MESH,
        )

    def s1_copy(m):
        return remote(s1buf.at[m], r1buf.at[m], s1_send.at[m], s1_recv.at[m], "dir", partner)

    def s2_copy(m, o):
        to = lax.rem(chip + o, chips)
        return remote(
            s2buf.at[m, to],
            r2buf.at[m, o],
            s2_send.at[m, o],
            s2_recv.at[m, o],
            "dir",
            to * 2 + core,
        )

    def row_slice(owner):
        return pl.ds(pl.multiple_of(owner * rows, rows), rows)

    def ag_copy(m, o):
        to = partner if o == 0 else lax.rem(chip + o, chips) * 2 + core
        piece = ugath.at[m, row_slice(me), :]
        return remote(piece, piece, ag_send.at[m, o], ag_recv.at[m, o], "dir", to)

    def fw_copy(m, o):
        owner = lax.rem(chip - o + chips, chips) * 2 + core
        piece = ugath.at[m, row_slice(owner), :]
        return remote(piece, piece, fw_send.at[m, o], ag_recv.at[m, chips + o - 1], "dir", partner)

    chunk = 32

    def phasors(m):
        gain_copy(m).wait()

        def one(i, _):
            at = pl.ds(pl.multiple_of(i * chunk, chunk), chunk)
            col = cols[m, at, :]
            lm = lm_ref[...]
            turns = col[:, 0:1] * lm[0:1] + col[:, 1:2] * lm[1:2]
            own = jnp.broadcast_to(col[:, 2:3], turns.shape)
            for d in range(1, local_dirs):
                own = jnp.where(dirs_ref[...] == d, col[:, 2 + d : 3 + d], own)
            turns = turns + own
            r = turns - jnp.round(turns)
            z = r * r
            amp = jnp.sqrt(flux_ref[...])
            sine = horner(SIN_POLY, z) * (r * amp)
            cosine = horner(COS_POLY, z) * amp
            g_re = gain[m, 0, at, :].astype(f32)
            g_im = gain[m, 1, at, :].astype(f32)
            re = (g_re * cosine - g_im * sine).astype(bf16)
            im = (g_re * sine + g_im * cosine).astype(bf16)
            left[m, at, :sources] = re
            left[m, at, sources:] = im
            re = re.astype(f32)
            im = im.astype(f32)
            mixed[m, at, :sources] = (re + im).astype(bf16)
            mixed[m, at, sources:] = (im - re).astype(bf16)
            return 0

        lax.fori_loop(0, stations // chunk, one, 0)

    def nt_dot(a, b):
        return lax.dot_general(a, b, (((1,), (1,)), ((), ())), preferred_element_type=f32)

    def partial_model(m):
        pfull[m] = nt_dot(mixed[m], left[m]).reshape(chips, 2, rows, stations)

        def one(j, _):
            s1buf[m, j] = pfull[m, j, 1 - core].astype(bf16)
            return 0

        lax.fori_loop(0, chips, one, 0)

    def chip_sum(m):
        s1_copy(m).wait_recv()

        def one(j, _):
            total = pfull[m, j, core] + r1buf[m, j].astype(f32)
            s2buf[m, j] = total.astype(bf16)
            return 0

        lax.fori_loop(0, chips, one, 0)
        for o in range(1, chips):
            s2_copy(m, o).start()
        qown[m] = pfull[m, chip, core] + r1buf[m, chip].astype(f32)

    def own_residual(m):
        total = qown[m]
        for o in range(1, chips):
            s2_copy(m, o).wait_recv()
            total = total + r2buf[m, o].astype(f32)
        row_ids = me * rows + lax.broadcasted_iota(jnp.int32, (rows, 128), 0)
        lane_ids = lax.broadcasted_iota(jnp.int32, (rows, 128), 1)
        for b in range(tiles):
            lanes = slice(b * 128, (b + 1) * 128)
            at = (m * tiles + b) * 2
            real = obs[pl.ds(at, rows, stride=count * tiles * 2), :]
            imag = obs[pl.ds(at + 1, rows, stride=count * tiles * 2), :]
            flag = flags[pl.ds(b * times + lax.rem(m, times), rows, stride=tiles * times), :]
            keep = jnp.where(row_ids == lane_ids + b * 128, 0, flag).astype(f32)
            value = keep * (real + imag - total[:, lanes] * scaling)
            own_res[m, :, lanes] = value
            ugath[m, row_slice(me), lanes] = value.astype(bf16)
        for o in list(range(1, chips)) + [0]:
            ag_copy(m, o).start()

    def forward(m):
        for o in range(1, chips):
            ag_copy(m, o).wait_recv()
            fw_copy(m, o).start()

    def direction_models(m):
        for d in range(local_dirs):
            mask = jnp.where(dirs_ref[...] == d, 1.0, 0.0).astype(bf16)
            mask = jnp.concatenate([mask, mask], axis=1)
            pdir[d] = nt_dot(left[m] * mask, mixed[m])

    def local_grad(m):
        ag_copy(m, 0).wait_recv()
        for o in range(1, chips):
            fw_copy(m, o).wait_recv()
        weight = scaling / ratio_ref[0, lax.div(m, times)]

        def one(i, carry):
            at = pl.ds(pl.multiple_of(i * chunk, chunk), chunk)
            u = ugath[m, at, :].astype(f32) * weight
            out = []
            for d in range(local_dirs):
                w = u * pdir[d, at, :]
                part = w[:, 0:128]
                for b in range(1, stations // 128):
                    part = part + w[:, b * 128 : (b + 1) * 128]
                rowacc[d, at, :] += part
                c = carry[d]
                for b in range(chunk // 8):
                    c = c + w[b * 8 : (b + 1) * 8]
                out.append(c)
            return tuple(out)

        init = tuple(colacc[d] for d in range(local_dirs))
        out = lax.fori_loop(0, stations // chunk, one, init)
        for d in range(local_dirs):
            colacc[d] = out[d]

    def step(s, _):
        @pl.when(s < count)
        def _():
            phasors(s)
            partial_model(s)

            @pl.when(s == 0)
            def _():
                pl.semaphore_wait(barrier, n_dir - 1 + n_freq - 1)
                for c in in_copies:
                    c.wait()

            s1_copy(s).start()

        @pl.when(jnp.logical_and(s >= 1, s < count + 1))
        def _():
            chip_sum(s - 1)

        @pl.when(jnp.logical_and(s >= 2, s < count + 2))
        def _():
            own_residual(s - 2)

        @pl.when(jnp.logical_and(s >= 3, s < count + 3))
        def _():
            forward(s - 3)

        @pl.when(s >= 4)
        def _():
            local_grad(s - 4)

        @pl.when(jnp.logical_and(s >= 3, s < count + 3))
        def _():
            direction_models(s - 3)

        return 0

    lax.fori_loop(0, count + 4, step, 0)

    mine = []
    for d in range(local_dirs):
        by_col = jnp.sum(colacc[d], axis=0, keepdims=True)
        by_row = jnp.sum(jnp.transpose(rowacc[d]), axis=0, keepdims=True)
        mine.append(by_col - by_row)
    mine.append(jnp.zeros((8 - local_dirs, stations), f32))
    gbuf[fme] = jnp.concatenate(mine, axis=0)

    def fr_copy(o):
        slot = gbuf.at[fme]
        return remote(
            slot, slot, fr_send.at[o], fr_recv.at[o], "freq", lax.rem(fme + o, n_freq)
        )

    for o in range(1, n_freq):
        fr_copy(o).start()

    group = 128 // rows
    lane0 = pl.multiple_of(lax.div(me, group) * 128, 128)
    sub0 = pl.multiple_of(lax.rem(me, group) * rows, rows)

    for m in range(count):
        for b in range(tiles):
            block = ugath[m, b * 128 : (b + 1) * 128, pl.ds(lane0, 128)].astype(f32)
            tbuf[m, b] = jnp.transpose(block)
            turned = tbuf[m, b, pl.ds(sub0, rows), :]
            own = own_res[m, :, b * 128 : (b + 1) * 128]
            at = (m * tiles + b) * 2
            resid_ref[pl.ds(at, rows, stride=count * tiles * 2), :] = (own + turned) * 0.5
            resid_ref[pl.ds(at + 1, rows, stride=count * tiles * 2), :] = (own - turned) * 0.5

    for o in range(1, n_freq):
        fr_copy(o).wait_recv()
    total = gbuf[0]
    for f in range(1, n_freq):
        total = total + gbuf[f]
    smooth = jnp.dot(
        total, kern[...], preferred_element_type=f32, precision=lax.Precision.HIGHEST
    )
    squares = smooth * smooth
    part = squares[:, 0:128]
    for b in range(1, stations // 128):
        part = part + squares[:, b * 128 : (b + 1) * 128]
    sqbuf[0] = part

    def sq_copy(o):
        return remote(
            sqbuf.at[0], sqbuf.at[o], sq_send.at[o], sq_recv.at[o], "dir", lax.rem(me + o, n_dir)
        )

    for o in range(1, n_dir):
        sq_copy(o).start()
    for o in range(1, n_dir):
        sq_copy(o).wait_recv()
        part = part + sqbuf[o]
    total_sq = jnp.sum(jnp.sum(part, axis=1, keepdims=True), axis=0, keepdims=True)
    scale = step_size * lax.rsqrt(total_sq / (local_dirs * n_dir * stations) + epsilon)
    updated_ref[...] = screen_ref[...] - smooth[:local_dirs] * scale

    def drain(m, _):
        s1_copy(m).wait_send()
        for o in range(1, chips):
            s2_copy(m, o).wait_send()
            fw_copy(m, o).wait_send()
        for o in range(chips):
            ag_copy(m, o).wait_send()
        return 0

    lax.fori_loop(0, count, drain, 0)
    for o in range(1, n_freq):
        fr_copy(o).wait_send()
    for o in range(1, n_dir):
        sq_copy(o).wait_send()


def body(
    observed,
    flags,
    screen,
    screen_kernel,
    station_uv,
    source_lm,
    source_flux,
    station_gain,
    source_direction,
    freq_ratio,
):
    n_dir = lax.axis_size("dir")
    n_freq = lax.axis_size("freq")
    local_dirs, stations = screen.shape
    sources = source_flux.shape[0]
    rows = observed.shape[0]
    channels = freq_ratio.shape[0]
    times = station_uv.shape[0]
    count = channels * times
    chips = n_dir // 2
    scaling = 1.0 / math.sqrt(sources * n_dir)

    tiles = stations // 128
    gain = station_gain.reshape(count, 2, stations, sources)
    obs = observed.reshape(rows, count, 2, tiles, 128)
    obs = jnp.transpose(obs, (0, 1, 3, 2, 4)).reshape(rows * count * tiles * 2, 128)
    flag_rows = jnp.transpose(flags.reshape(rows, times, tiles, 128), (0, 2, 1, 3))
    flag_rows = flag_rows.reshape(rows * tiles * times, 128)

    vmem = pl.BlockSpec(memory_space=pltpu.VMEM)
    hbm = pl.BlockSpec(memory_space=pl.ANY)
    dma = pltpu.SemaphoreType.DMA
    residual, updated = pl.pallas_call(
        functools.partial(kernel, n_dir, n_freq, scaling),
        out_shape=(
            jax.ShapeDtypeStruct((rows * count * tiles * 2, 128), f32),
            jax.ShapeDtypeStruct((local_dirs, stations), f32),
        ),
        in_specs=[
            pl.BlockSpec(memory_space=pltpu.SMEM),
            hbm,
            vmem,
            vmem,
            vmem,
            vmem,
            hbm,
            hbm,
            vmem,
            hbm,
        ],
        out_specs=(vmem, vmem),
        scratch_shapes=[
            pltpu.VMEM((count, 2, stations, sources), bf16),
            pltpu.VMEM((rows * count * tiles * 2, 128), f32),
            pltpu.VMEM((rows * tiles * times, 128), jnp.int32),
            pltpu.VMEM((stations, stations), f32),
            pltpu.VMEM((count, stations, 8), f32),
            pltpu.VMEM((count, rows, stations), f32),
            pltpu.VMEM((count, stations, 2 * sources), bf16),
            pltpu.VMEM((count, stations, 2 * sources), bf16),
            pltpu.VMEM((count, chips, 2, rows, stations), f32),
            pltpu.VMEM((local_dirs, stations, stations), f32),
            pltpu.VMEM((count, chips, rows, stations), bf16),
            pltpu.VMEM((count, chips, rows, stations), bf16),
            pltpu.VMEM((count, chips, rows, stations), bf16),
            pltpu.VMEM((count, rows, stations), f32),
            pltpu.VMEM((count, chips, rows, stations), bf16),
            pltpu.VMEM((count, stations, stations), bf16),
            pltpu.VMEM((local_dirs, stations, 128), f32),
            pltpu.VMEM((local_dirs, 8, stations), f32),
            pltpu.VMEM((n_freq, 8, stations), f32),
            pltpu.VMEM((n_dir, 8, 128), f32),
            pltpu.VMEM((count, tiles, 128, 128), f32),
            dma((count,)),
            dma((3,)),
            dma((count,)),
            dma((count,)),
            dma((count, chips)),
            dma((count, chips)),
            dma((count, chips)),
            dma((count, 2 * chips)),
            dma((count, chips)),
            dma((n_freq,)),
            dma((n_freq,)),
            dma((n_dir,)),
            dma((n_dir,)),
        ],
        compiler_params=pltpu.CompilerParams(
            collective_id=0, has_side_effects=True, vmem_limit_bytes=60 * 1024 * 1024
        ),
        name="calibrate",
    )(
        freq_ratio[None],
        gain,
        station_uv,
        source_lm,
        source_flux[None],
        source_direction[None],
        obs,
        flag_rows,
        screen,
        screen_kernel,
    )
    residual = residual.reshape(rows, count, tiles, 2, 128)
    residual = jnp.transpose(residual, (0, 1, 3, 2, 4))
    return (residual.reshape(observed.shape), updated)


def solution(mesh):
    placed = (
        P("dir", "freq", None, None, None),
        P("dir", None, None),
        P("dir", None),
        P(),
        P(),
        P(None, "dir"),
        P("dir"),
        P("freq", None, None, None, "dir"),
        P("dir"),
        P("freq"),
    )
    return jax.shard_map(
        body,
        mesh=mesh,
        in_specs=placed,
        out_specs=(P("dir", "freq", None, None, None), P("dir", None)),
        check_vma=False,
    )
```

```python
import functools
import math

import jax
import jax.numpy as jnp
from jax import lax
from jax.experimental import pallas as pl
from jax.experimental.pallas import tpu as pltpu
from jax.sharding import PartitionSpec as P

step_size = 0.3
epsilon = 1e-06
MESH = pl.DeviceIdType.MESH
f32 = jnp.float32
bf16 = jnp.bfloat16

SIN_POLY = (6.283185272722381, -41.341697068949564, 81.60502462236155, -76.70155117323625, 42.01616580115987, -14.868610927638132, 3.19969357384433)
COS_POLY = (0.9999999891722522, -19.739204532086525, 64.93911898351571, -85.45016554378464, 60.16783168053616, -25.968313120273056, 6.5296101719799085)


def horner(coefs, z):
    total = jnp.full_like(z, coefs[-1])
    for c in coefs[-2::-1]:
        total = total * z + c
    return total


def kernel(
    n_dir,
    n_freq,
    scaling,
    ratio_ref,
    gain_hbm,
    uv_ref,
    lm_ref,
    flux_ref,
    dirs_ref,
    obs_hbm,
    flags_hbm,
    screen_ref,
    kern_hbm,
    resid_ref,
    updated_ref,
    gain,
    obs,
    flags,
    kern,
    cols,
    own_res,
    left,
    mixed,
    pfull,
    pdir,
    s1buf,
    r1buf,
    s2buf,
    qown,
    r2buf,
    ugath,
    rowacc,
    colacc,
    gbuf,
    sqbuf,
    tbuf,
    gain_sem,
    in_sem,
    s1_send,
    s1_recv,
    s2_send,
    s2_recv,
    ag_send,
    ag_recv,
    fw_send,
    fr_send,
    fr_recv,
    sq_send,
    sq_recv,
):
    count, _, stations, sources = gain.shape
    local_dirs = pdir.shape[1]
    times = uv_ref.shape[0]
    rows = own_res.shape[1]
    tiles = stations // 128
    chips = n_dir // 2
    me = lax.axis_index("dir")
    fme = lax.axis_index("freq")
    core = lax.rem(me, 2)
    chip = lax.div(me, 2)
    partner = chip * 2 + 1 - core

    def gain_copy(m):
        return pltpu.make_async_copy(gain_hbm.at[m], gain.at[m], gain_sem.at[m])

    for m in range(count):
        gain_copy(m).start()
    in_copies = [
        pltpu.make_async_copy(obs_hbm, obs, in_sem.at[0]),
        pltpu.make_async_copy(flags_hbm, flags, in_sem.at[1]),
        pltpu.make_async_copy(kern_hbm, kern, in_sem.at[2]),
    ]
    for c in in_copies:
        c.start()

    barrier = pltpu.get_barrier_semaphore()
    for o in range(1, n_dir):
        pl.semaphore_signal(
            barrier, inc=1, device_id={"dir": lax.rem(me + o, n_dir)}, device_id_type=MESH
        )
    for o in range(1, n_freq):
        pl.semaphore_signal(
            barrier, inc=1, device_id={"freq": lax.rem(fme + o, n_freq)}, device_id_type=MESH
        )

    for m in range(count):
        ratio = ratio_ref[0, m // times]
        parts = [uv_ref[m % times] * ratio, screen_ref[...] / (ratio * (2.0 * math.pi))]
        parts.append(jnp.zeros((8 - 2 - local_dirs, stations), f32))
        cols[m] = jnp.transpose(jnp.concatenate(parts, axis=0))
    rowacc[...] = jnp.zeros_like(rowacc)
    colacc[...] = jnp.zeros_like(colacc)

    def remote(src, dst, send, recv, axis, where):
        return pltpu.make_async_remote_copy(
            src_ref=src,
            dst_ref=dst,
            send_sem=send,
            recv_sem=recv,
            device_id={axis: where},
            device_id_type=MESH,
        )

    def s1_copy(m):
        return remote(s1buf.at[m], r1buf.at[m], s1_send.at[m], s1_recv.at[m], "dir", partner)

    def s2_copy(m, o):
        to = lax.rem(chip + o, chips)
        return remote(
            s2buf.at[m, to],
            r2buf.at[m, o],
            s2_send.at[m, o],
            s2_recv.at[m, o],
            "dir",
            to * 2 + core,
        )

    def row_slice(owner):
        return pl.ds(pl.multiple_of(owner * rows, rows), rows)

    def ag_copy(m, o):
        to = partner if o == 0 else lax.rem(chip + o, chips) * 2 + core
        piece = ugath.at[m, row_slice(me), :]
        return remote(piece, piece, ag_send.at[m, o], ag_recv.at[m, o], "dir", to)

    def fw_copy(m, o):
        owner = lax.rem(chip - o + chips, chips) * 2 + core
        piece = ugath.at[m, row_slice(owner), :]
        return remote(piece, piece, fw_send.at[m, o], ag_recv.at[m, chips + o - 1], "dir", partner)

    chunk = 32

    def phasors(m):
        gain_copy(m).wait()

        def one(i, _):
            at = pl.ds(pl.multiple_of(i * chunk, chunk), chunk)
            col = cols[m, at, :]
            lm = lm_ref[...]
            turns = col[:, 0:1] * lm[0:1] + col[:, 1:2] * lm[1:2]
            own = jnp.broadcast_to(col[:, 2:3], turns.shape)
            for d in range(1, local_dirs):
                own = jnp.where(dirs_ref[...][None] == d, col[:, 2 + d : 3 + d], own)
            turns = turns + own
            r = turns - jnp.round(turns)
            z = r * r
            amp = jnp.sqrt(flux_ref[...])[None]
            sine = horner(SIN_POLY, z) * (r * amp)
            cosine = horner(COS_POLY, z) * amp
            g_re = gain[m, 0, at, :].astype(f32)
            g_im = gain[m, 1, at, :].astype(f32)
            re = (g_re * cosine - g_im * sine).astype(bf16)
            im = (g_re * sine + g_im * cosine).astype(bf16)
            left[m, at, :sources] = re
            left[m, at, sources:] = im
            re = re.astype(f32)
            im = im.astype(f32)
            mixed[m, at, :sources] = (re + im).astype(bf16)
            mixed[m, at, sources:] = (im - re).astype(bf16)
            return 0

        lax.fori_loop(0, stations // chunk, one, 0)

    def nt_dot(a, b):
        return lax.dot_general(a, b, (((1,), (1,)), ((), ())), preferred_element_type=f32)

    def partial_model(m):
        pfull[m] = nt_dot(mixed[m], left[m]).reshape(chips, 2, rows, stations)

        def one(j, _):
            s1buf[m, j] = pfull[m, j, 1 - core].astype(bf16)
            return 0

        lax.fori_loop(0, chips, one, 0)

    def chip_sum(m):
        s1_copy(m).wait_recv()

        def one(j, _):
            total = pfull[m, j, core] + r1buf[m, j].astype(f32)
            s2buf[m, j] = total.astype(bf16)
            return 0

        lax.fori_loop(0, chips, one, 0)
        for o in range(1, chips):
            s2_copy(m, o).start()
        qown[m] = pfull[m, chip, core] + r1buf[m, chip].astype(f32)

    def own_residual(m):
        total = qown[m]
        for o in range(1, chips):
            s2_copy(m, o).wait_recv()
            total = total + r2buf[m, o].astype(f32)
        row_ids = me * rows + lax.broadcasted_iota(jnp.int32, (rows, 128), 0)
        lane_ids = lax.broadcasted_iota(jnp.int32, (rows, 128), 1)
        for b in range(tiles):
            lanes = slice(b * 128, (b + 1) * 128)
            at = (m * tiles + b) * 2
            real = obs[pl.ds(at, rows, stride=count * tiles * 2), :]
            imag = obs[pl.ds(at + 1, rows, stride=count * tiles * 2), :]
            flag = flags[pl.ds(b * times + lax.rem(m, times), rows, stride=tiles * times), :]
            keep = jnp.where(row_ids == lane_ids + b * 128, 0, flag).astype(f32)
            value = keep * (real + imag - total[:, lanes] * scaling)
            own_res[m, :, lanes] = value
            ugath[m, row_slice(me), lanes] = value.astype(bf16)
        for o in list(range(1, chips)) + [0]:
            ag_copy(m, o).start()

    def forward(m):
        for o in range(1, chips):
            ag_copy(m, o).wait_recv()
            fw_copy(m, o).start()

    def direction_models(m):
        for d in range(local_dirs):
            mask = jnp.where(dirs_ref[...][None] == d, 1.0, 0.0).astype(bf16)
            mask = jnp.concatenate([mask, mask], axis=1)
            pdir[m, d] = nt_dot(left[m] * mask, mixed[m])

    def local_grad(m):
        ag_copy(m, 0).wait_recv()
        for o in range(1, chips):
            fw_copy(m, o).wait_recv()
        weight = scaling / ratio_ref[0, lax.div(m, times)]

        def one(i, carry):
            at = pl.ds(pl.multiple_of(i * chunk, chunk), chunk)
            u = ugath[m, at, :].astype(f32) * weight
            out = []
            for d in range(local_dirs):
                w = u * pdir[m, d, at, :]
                part = w[:, 0:128]
                for b in range(1, stations // 128):
                    part = part + w[:, b * 128 : (b + 1) * 128]
                rowacc[d, at, :] += part
                c = carry[d]
                for b in range(chunk // 8):
                    c = c + w[b * 8 : (b + 1) * 8]
                out.append(c)
            return tuple(out)

        init = tuple(colacc[d] for d in range(local_dirs))
        out = lax.fori_loop(0, stations // chunk, one, init)
        for d in range(local_dirs):
            colacc[d] = out[d]

    group = 128 // rows
    lane0 = pl.multiple_of(lax.div(me, group) * 128, 128)
    sub0 = pl.multiple_of(lax.rem(me, group) * rows, rows)

    def mirror(m):
        for b in range(tiles):
            block = ugath[m, b * 128 : (b + 1) * 128, pl.ds(lane0, 128)].astype(f32)
            tbuf[m, b] = jnp.transpose(block)
        for b in range(tiles):
            turned = tbuf[m, b, pl.ds(sub0, rows), :]
            own = own_res[m, :, b * 128 : (b + 1) * 128]
            at = (m * tiles + b) * 2
            resid_ref[pl.ds(at, rows, stride=count * tiles * 2), :] = (own + turned) * 0.5
            resid_ref[pl.ds(at + 1, rows, stride=count * tiles * 2), :] = (own - turned) * 0.5

    lag = min(3, count - 1)

    def build(s, _):
        phasors(s)
        partial_model(s)

        @pl.when(s == 0)
        def _():
            pl.semaphore_wait(barrier, n_dir - 1 + n_freq - 1)
            for c in in_copies:
                c.wait()

        s1_copy(s).start()

        @pl.when(s >= 1)
        def _():
            chip_sum(s - 1)

        @pl.when(s >= lag)
        def _():
            own_residual(s - lag)

        return 0

    lax.fori_loop(0, count, build, 0)
    chip_sum(count - 1)

    def spread(j, _):
        @pl.when(j < lag)
        def _():
            own_residual(j + count - lag)

        @pl.when(j < count)
        def _():
            direction_models(j)

        @pl.when(jnp.logical_and(j >= 1, j < count + 1))
        def _():
            forward(j - 1)

        @pl.when(j >= 2)
        def _():
            local_grad(j - 2)

            @pl.when(j < count + 1)
            def _():
                mirror(j - 2)

        return 0

    lax.fori_loop(0, count + 2, spread, 0)

    mine = []
    for d in range(local_dirs):
        by_col = jnp.sum(colacc[d], axis=0, keepdims=True)
        by_row = jnp.sum(jnp.transpose(rowacc[d]), axis=0, keepdims=True)
        mine.append(by_col - by_row)
    mine.append(jnp.zeros((8 - local_dirs, stations), f32))
    gbuf[fme] = jnp.concatenate(mine, axis=0)

    def fr_copy(o):
        slot = gbuf.at[fme]
        return remote(
            slot, slot, fr_send.at[o], fr_recv.at[o], "freq", lax.rem(fme + o, n_freq)
        )

    for o in range(1, n_freq):
        fr_copy(o).start()

    mirror(count - 1)

    for o in range(1, n_freq):
        fr_copy(o).wait_recv()
    total = gbuf[0]
    for f in range(1, n_freq):
        total = total + gbuf[f]
    smooth = jnp.dot(
        total, kern[...], preferred_element_type=f32, precision=lax.Precision.HIGHEST
    )
    squares = smooth * smooth
    part = squares[:, 0:128]
    for b in range(1, stations // 128):
        part = part + squares[:, b * 128 : (b + 1) * 128]
    sqbuf[0] = part

    def sq_copy(o):
        return remote(
            sqbuf.at[0], sqbuf.at[o], sq_send.at[o], sq_recv.at[o], "dir", lax.rem(me + o, n_dir)
        )

    for o in range(1, n_dir):
        sq_copy(o).start()
    for o in range(1, n_dir):
        sq_copy(o).wait_recv()
        part = part + sqbuf[o]
    total_sq = jnp.sum(jnp.sum(part, axis=1, keepdims=True), axis=0, keepdims=True)
    scale = step_size * lax.rsqrt(total_sq / (local_dirs * n_dir * stations) + epsilon)
    updated_ref[...] = screen_ref[...] - smooth[:local_dirs] * scale

    def drain(m, _):
        s1_copy(m).wait_send()
        for o in range(1, chips):
            s2_copy(m, o).wait_send()
            fw_copy(m, o).wait_send()
        for o in range(chips):
            ag_copy(m, o).wait_send()
        return 0

    lax.fori_loop(0, count, drain, 0)
    for o in range(1, n_freq):
        fr_copy(o).wait_send()
    for o in range(1, n_dir):
        sq_copy(o).wait_send()


def body(
    observed,
    flags,
    screen,
    screen_kernel,
    station_uv,
    source_lm,
    source_flux,
    station_gain,
    source_direction,
    freq_ratio,
):
    n_dir = lax.axis_size("dir")
    n_freq = lax.axis_size("freq")
    local_dirs, stations = screen.shape
    sources = source_flux.shape[0]
    rows = observed.shape[0]
    channels = freq_ratio.shape[0]
    times = station_uv.shape[0]
    count = channels * times
    chips = n_dir // 2
    scaling = 1.0 / math.sqrt(sources * n_dir)

    tiles = stations // 128
    gain = station_gain.reshape(count, 2, stations, sources)
    obs = observed.reshape(rows, count, 2, tiles, 128)
    obs = jnp.transpose(obs, (0, 1, 3, 2, 4)).reshape(rows * count * tiles * 2, 128)
    flag_rows = jnp.transpose(flags.reshape(rows, times, tiles, 128), (0, 2, 1, 3))
    flag_rows = flag_rows.reshape(rows * tiles * times, 128)

    vmem = pl.BlockSpec(memory_space=pltpu.VMEM)
    hbm = pl.BlockSpec(memory_space=pl.ANY)
    dma = pltpu.SemaphoreType.DMA
    residual, updated = pl.pallas_call(
        functools.partial(kernel, n_dir, n_freq, scaling),
        out_shape=(
            jax.ShapeDtypeStruct((rows * count * tiles * 2, 128), f32),
            jax.ShapeDtypeStruct((local_dirs, stations), f32),
        ),
        in_specs=[
            pl.BlockSpec(memory_space=pltpu.SMEM),
            hbm,
            vmem,
            vmem,
            vmem,
            vmem,
            hbm,
            hbm,
            vmem,
            hbm,
        ],
        out_specs=(vmem, vmem),
        scratch_shapes=[
            pltpu.VMEM((count, 2, stations, sources), bf16),
            pltpu.VMEM((rows * count * tiles * 2, 128), f32),
            pltpu.VMEM((rows * tiles * times, 128), jnp.int32),
            pltpu.VMEM((stations, stations), f32),
            pltpu.VMEM((count, stations, 8), f32),
            pltpu.VMEM((count, rows, stations), f32),
            pltpu.VMEM((count, stations, 2 * sources), bf16),
            pltpu.VMEM((count, stations, 2 * sources), bf16),
            pltpu.VMEM((count, chips, 2, rows, stations), f32),
            pltpu.VMEM((count, local_dirs, stations, stations), f32),
            pltpu.VMEM((count, chips, rows, stations), bf16),
            pltpu.VMEM((count, chips, rows, stations), bf16),
            pltpu.VMEM((count, chips, rows, stations), bf16),
            pltpu.VMEM((count, rows, stations), f32),
            pltpu.VMEM((count, chips, rows, stations), bf16),
            pltpu.VMEM((count, stations, stations), bf16),
            pltpu.VMEM((local_dirs, stations, 128), f32),
            pltpu.VMEM((local_dirs, 8, stations), f32),
            pltpu.VMEM((n_freq, 8, stations), f32),
            pltpu.VMEM((n_dir, 8, 128), f32),
            pltpu.VMEM((count, tiles, 128, 128), f32),
            dma((count,)),
            dma((3,)),
            dma((count,)),
            dma((count,)),
            dma((count, chips)),
            dma((count, chips)),
            dma((count, chips)),
            dma((count, 2 * chips)),
            dma((count, chips)),
            dma((n_freq,)),
            dma((n_freq,)),
            dma((n_dir,)),
            dma((n_dir,)),
        ],
        compiler_params=pltpu.CompilerParams(
            collective_id=0, has_side_effects=True, vmem_limit_bytes=60 * 1024 * 1024
        ),
        name="calibrate",
    )(
        freq_ratio[None],
        gain,
        station_uv,
        source_lm,
        source_flux,
        source_direction,
        obs,
        flag_rows,
        screen,
        screen_kernel,
    )
    residual = residual.reshape(rows, count, tiles, 2, 128)
    residual = jnp.transpose(residual, (0, 1, 3, 2, 4))
    return (residual.reshape(observed.shape), updated)


def solution(mesh):
    placed = (
        P("dir", "freq", None, None, None),
        P("dir", None, None),
        P("dir", None),
        P(),
        P(),
        P(None, "dir"),
        P("dir"),
        P("freq", None, None, None, "dir"),
        P("dir"),
        P("freq"),
    )
    return jax.shard_map(
        body,
        mesh=mesh,
        in_specs=placed,
        out_specs=(P("dir", "freq", None, None, None), P("dir", None)),
        check_vma=False,
    )
```

```python
import functools
import math

import jax
import jax.numpy as jnp
from jax import lax
from jax.experimental import pallas as pl
from jax.experimental.pallas import tpu as pltpu
from jax.sharding import PartitionSpec as P

step_size = 0.3
epsilon = 1e-06
MESH = pl.DeviceIdType.MESH
f32 = jnp.float32
bf16 = jnp.bfloat16

SIN_POLY = (6.283182818548967, -41.34142139850843, 81.59618386869336, -76.58010048367296, 41.20539468675213, -12.27126208031411)
COS_POLY = (0.9999992215699194, -19.738982515967884, 64.92872660466796, -85.27239684712507, 58.79403796941139, -21.076780928848983)


def horner(coefs, z):
    total = jnp.full_like(z, coefs[-1])
    for c in coefs[-2::-1]:
        total = total * z + c
    return total


def kernel(
    n_dir,
    n_freq,
    scaling,
    ratio_ref,
    gain_hbm,
    uv_ref,
    lm_ref,
    flux_ref,
    dirs_ref,
    obs_hbm,
    flags_hbm,
    screen_ref,
    kern_hbm,
    resid_ref,
    updated_ref,
    gain,
    obs,
    flags,
    kern,
    cols,
    own_res,
    left,
    mixed,
    pfull,
    pdir,
    s1buf,
    r1buf,
    s2buf,
    qown,
    r2buf,
    ugath,
    rowacc,
    colacc,
    gbuf,
    sqbuf,
    tbuf,
    gain_sem,
    in_sem,
    s1_send,
    s1_recv,
    s2_send,
    s2_recv,
    ag_send,
    ag_recv,
    fw_send,
    fr_send,
    fr_recv,
    sq_send,
    sq_recv,
):
    count, _, stations, sources = gain.shape
    local_dirs = pdir.shape[1]
    times = uv_ref.shape[0]
    rows = own_res.shape[1]
    tiles = stations // 128
    chips = n_dir // 2
    me = lax.axis_index("dir")
    fme = lax.axis_index("freq")
    core = lax.rem(me, 2)
    chip = lax.div(me, 2)
    partner = chip * 2 + 1 - core
    square = chips == 4
    across = chip + 1 - 2 * lax.rem(chip, 2)
    along = lax.rem(chip + 2, 4)
    first = across + core * (along - across)
    second = along + core * (across - along)
    corner = 3 - chip

    def gain_copy(m):
        return pltpu.make_async_copy(gain_hbm.at[m], gain.at[m], gain_sem.at[m])

    for m in range(count):
        gain_copy(m).start()
    in_copies = [
        pltpu.make_async_copy(obs_hbm, obs, in_sem.at[0]),
        pltpu.make_async_copy(flags_hbm, flags, in_sem.at[1]),
        pltpu.make_async_copy(kern_hbm, kern, in_sem.at[2]),
    ]
    for c in in_copies:
        c.start()

    barrier = pltpu.get_barrier_semaphore()
    for o in range(1, n_dir):
        pl.semaphore_signal(
            barrier, inc=1, device_id={"dir": lax.rem(me + o, n_dir)}, device_id_type=MESH
        )
    for o in range(1, n_freq):
        pl.semaphore_signal(
            barrier, inc=1, device_id={"freq": lax.rem(fme + o, n_freq)}, device_id_type=MESH
        )

    for m in range(count):
        ratio = ratio_ref[0, m // times]
        parts = [uv_ref[m % times] * ratio, screen_ref[...] / (ratio * (2.0 * math.pi))]
        parts.append(jnp.zeros((8 - 2 - local_dirs, stations), f32))
        cols[m] = jnp.transpose(jnp.concatenate(parts, axis=0))
    rowacc[...] = jnp.zeros_like(rowacc)
    colacc[...] = jnp.zeros_like(colacc)

    def remote(src, dst, send, recv, axis, where):
        return pltpu.make_async_remote_copy(
            src_ref=src,
            dst_ref=dst,
            send_sem=send,
            recv_sem=recv,
            device_id={axis: where},
            device_id_type=MESH,
        )

    def s1_copy(m):
        return remote(s1buf.at[m], r1buf.at[m], s1_send.at[m], s1_recv.at[m], "dir", partner)

    def s2_copy(m, o):
        if square:
            src, dst = s2buf.at[m, pl.ds(0, 2)], r2buf.at[m, pl.ds(0, 2)]
            if o == 2:
                src, dst = s2buf.at[m, 2], r2buf.at[m, 2]
            to = first if o == 1 else second
        else:
            to = lax.rem(chip + o, chips)
            src, dst = s2buf.at[m, to], r2buf.at[m, o]
        return remote(src, dst, s2_send.at[m, o], s2_recv.at[m, o], "dir", to * 2 + core)

    s2_count = 3 if square else chips

    def row_slice(owner):
        return pl.ds(pl.multiple_of(owner * rows, rows), rows)

    def source_chip(o):
        if square:
            return (chip, first, second, corner)[o]
        return lax.rem(chip - o + chips, chips)

    def ag_copy(m, o):
        owner = chip
        if square:
            to = (None, first, second, second)[o]
            owner = first if o == 3 else chip
        else:
            to = lax.rem(chip + o, chips)
        to = partner if o == 0 else to * 2 + core
        piece = ugath.at[m, row_slice(owner * 2 + core), :]
        return remote(piece, piece, ag_send.at[m, o], ag_recv.at[m, o], "dir", to)

    def fw_copy(m, o):
        piece = ugath.at[m, row_slice(source_chip(o) * 2 + core), :]
        return remote(piece, piece, fw_send.at[m, o], ag_recv.at[m, chips + o - 1], "dir", partner)

    chunk = 32

    def phasors(m):
        gain_copy(m).wait()

        def one(i, _):
            at = pl.ds(pl.multiple_of(i * chunk, chunk), chunk)
            col = cols[m, at, :]
            lm = lm_ref[...]
            turns = col[:, 0:1] * lm[0:1] + col[:, 1:2] * lm[1:2]
            own = jnp.broadcast_to(col[:, 2:3], turns.shape)
            for d in range(1, local_dirs):
                own = jnp.where(dirs_ref[...][None] == d, col[:, 2 + d : 3 + d], own)
            turns = turns + own
            r = turns - jnp.round(turns)
            z = r * r
            amp = jnp.sqrt(flux_ref[...])[None]
            sine = horner(SIN_POLY, z) * (r * amp)
            cosine = horner(COS_POLY, z) * amp
            g_re = gain[m, 0, at, :].astype(f32)
            g_im = gain[m, 1, at, :].astype(f32)
            re = (g_re * cosine - g_im * sine).astype(bf16)
            im = (g_re * sine + g_im * cosine).astype(bf16)
            left[m, at, :sources] = re
            left[m, at, sources:] = im
            mixed[m, at, :sources] = re + im
            mixed[m, at, sources:] = im - re
            return 0

        lax.fori_loop(0, stations // chunk, one, 0)

    def nt_dot(a, b):
        return lax.dot_general(a, b, (((1,), (1,)), ((), ())), preferred_element_type=f32)

    def partial_model(m):
        pfull[m] = nt_dot(mixed[m], left[m]).reshape(chips, 2, rows, stations)

        def one(j, _):
            s1buf[m, j] = pfull[m, j, 1 - core].astype(bf16)
            return 0

        lax.fori_loop(0, chips, one, 0)

    def core_sum(m, j):
        return pfull[m, j, core] + r1buf[m, j].astype(f32)

    def chip_sum(m):
        s1_copy(m).wait_recv()
        if square:
            s2buf[m, 0] = core_sum(m, first).astype(bf16)
            s2buf[m, 1] = core_sum(m, corner).astype(bf16)
            s2_copy(m, 1).start()
            qown[m, 0] = core_sum(m, chip)
            qown[m, 1] = core_sum(m, second)
        else:
            for j in range(chips):
                s2buf[m, j] = core_sum(m, j).astype(bf16)
            for o in range(1, chips):
                s2_copy(m, o).start()
            qown[m, 0] = core_sum(m, chip)

    def square_sum(m):
        s2_copy(m, 1).wait_recv()
        s2buf[m, 2] = (qown[m, 1] + r2buf[m, 1].astype(f32)).astype(bf16)
        s2_copy(m, 2).start()
        qown[m, 0] = qown[m, 0] + r2buf[m, 0].astype(f32)

    def own_residual(m):
        total = qown[m, 0]
        for o in [2] if square else range(1, chips):
            s2_copy(m, o).wait_recv()
            total = total + r2buf[m, o].astype(f32)
        row_ids = me * rows + lax.broadcasted_iota(jnp.int32, (rows, 128), 0)
        lane_ids = lax.broadcasted_iota(jnp.int32, (rows, 128), 1)
        for b in range(tiles):
            lanes = slice(b * 128, (b + 1) * 128)
            at = (m * tiles + b) * 2
            real = obs[pl.ds(at, rows, stride=count * tiles * 2), :]
            imag = obs[pl.ds(at + 1, rows, stride=count * tiles * 2), :]
            flag = flags[pl.ds(b * times + lax.rem(m, times), rows, stride=tiles * times), :]
            keep = jnp.where(row_ids == lane_ids + b * 128, 0, flag).astype(f32)
            value = keep * (real + imag - total[:, lanes] * scaling)
            own_res[m, :, lanes] = value
            ugath[m, row_slice(me), lanes] = value.astype(bf16)
        for o in [1, 2, 0] if square else list(range(1, chips)) + [0]:
            ag_copy(m, o).start()

    def relay(m):
        ag_copy(m, 1).wait_recv()
        ag_copy(m, 3).start()
        fw_copy(m, 1).start()
        ag_copy(m, 2).wait_recv()
        fw_copy(m, 2).start()

    def forward(m):
        for o in [3] if square else range(1, chips):
            ag_copy(m, o).wait_recv()
            fw_copy(m, o).start()

    def direction_models(m):
        for d in range(local_dirs):
            mask = jnp.where(dirs_ref[...][None] == d, 1.0, 0.0).astype(bf16)
            mask = jnp.concatenate([mask, mask], axis=1)
            pdir[m, d] = nt_dot(left[m] * mask, mixed[m])

    def local_grad(m):
        ag_copy(m, 0).wait_recv()
        for o in range(1, chips):
            fw_copy(m, o).wait_recv()
        weight = scaling / ratio_ref[0, lax.div(m, times)]

        def one(i, carry):
            at = pl.ds(pl.multiple_of(i * chunk, chunk), chunk)
            u = ugath[m, at, :].astype(f32) * weight
            out = []
            for d in range(local_dirs):
                w = u * pdir[m, d, at, :]
                part = w[:, 0:128]
                for b in range(1, stations // 128):
                    part = part + w[:, b * 128 : (b + 1) * 128]
                rowacc[d, at, :] += part
                c = carry[d]
                for b in range(chunk // 8):
                    c = c + w[b * 8 : (b + 1) * 8]
                out.append(c)
            return tuple(out)

        init = tuple(colacc[d] for d in range(local_dirs))
        out = lax.fori_loop(0, stations // chunk, one, init)
        for d in range(local_dirs):
            colacc[d] = out[d]

    group = 128 // rows
    lane0 = pl.multiple_of(lax.div(me, group) * 128, 128)
    sub0 = pl.multiple_of(lax.rem(me, group) * rows, rows)

    def mirror(m):
        for b in range(tiles):
            block = ugath[m, b * 128 : (b + 1) * 128, pl.ds(lane0, 128)].astype(f32)
            tbuf[m, b] = jnp.transpose(block)
        for b in range(tiles):
            turned = tbuf[m, b, pl.ds(sub0, rows), :]
            own = own_res[m, :, b * 128 : (b + 1) * 128]
            at = (m * tiles + b) * 2
            resid_ref[pl.ds(at, rows, stride=count * tiles * 2), :] = (own + turned) * 0.5
            resid_ref[pl.ds(at + 1, rows, stride=count * tiles * 2), :] = (own - turned) * 0.5

    def step(s, _):
        def stage(lag, run):
            @pl.when(jnp.logical_and(s >= lag, s < count + lag))
            def _():
                run(s - lag)

        @pl.when(s < count)
        def _():
            phasors(s)
            partial_model(s)

            @pl.when(s == 0)
            def _():
                pl.semaphore_wait(barrier, n_dir - 1 + n_freq - 1)
                for c in in_copies:
                    c.wait()

            s1_copy(s).start()

        stage(1, chip_sum)
        if square:
            stage(2, square_sum)
        stage(3, own_residual)
        if square:
            stage(5, relay)
        stage(6, forward)
        stage(7, local_grad)
        stage(4, direction_models)

        @pl.when(jnp.logical_and(s >= 7, s < count + 6))
        def _():
            mirror(s - 7)

        return 0

    lax.fori_loop(0, count + 7, step, 0)

    mine = []
    for d in range(local_dirs):
        by_col = jnp.sum(colacc[d], axis=0, keepdims=True)
        by_row = jnp.sum(jnp.transpose(rowacc[d]), axis=0, keepdims=True)
        mine.append(by_col - by_row)
    mine.append(jnp.zeros((8 - local_dirs, stations), f32))
    gbuf[fme] = jnp.concatenate(mine, axis=0)

    def fr_copy(o):
        slot = gbuf.at[fme]
        return remote(
            slot, slot, fr_send.at[o], fr_recv.at[o], "freq", lax.rem(fme + o, n_freq)
        )

    for o in range(1, n_freq):
        fr_copy(o).start()

    mirror(count - 1)

    for o in range(1, n_freq):
        fr_copy(o).wait_recv()
    total = gbuf[0]
    for f in range(1, n_freq):
        total = total + gbuf[f]
    smooth = jnp.dot(
        total, kern[...], preferred_element_type=f32, precision=lax.Precision.HIGHEST
    )
    squares = smooth * smooth
    part = squares[:, 0:128]
    for b in range(1, stations // 128):
        part = part + squares[:, b * 128 : (b + 1) * 128]
    sqbuf[0] = part

    def sq_copy(o):
        return remote(
            sqbuf.at[0], sqbuf.at[o], sq_send.at[o], sq_recv.at[o], "dir", lax.rem(me + o, n_dir)
        )

    for o in range(1, n_dir):
        sq_copy(o).start()
    for o in range(1, n_dir):
        sq_copy(o).wait_recv()
        part = part + sqbuf[o]
    total_sq = jnp.sum(jnp.sum(part, axis=1, keepdims=True), axis=0, keepdims=True)
    scale = step_size * lax.rsqrt(total_sq / (local_dirs * n_dir * stations) + epsilon)
    updated_ref[...] = screen_ref[...] - smooth[:local_dirs] * scale

    def drain(m, _):
        s1_copy(m).wait_send()
        for o in range(1, s2_count):
            s2_copy(m, o).wait_send()
        for o in range(1, chips):
            fw_copy(m, o).wait_send()
        for o in range(chips):
            ag_copy(m, o).wait_send()
        return 0

    lax.fori_loop(0, count, drain, 0)
    for o in range(1, n_freq):
        fr_copy(o).wait_send()
    for o in range(1, n_dir):
        sq_copy(o).wait_send()


def body(
    observed,
    flags,
    screen,
    screen_kernel,
    station_uv,
    source_lm,
    source_flux,
    station_gain,
    source_direction,
    freq_ratio,
):
    n_dir = lax.axis_size("dir")
    n_freq = lax.axis_size("freq")
    local_dirs, stations = screen.shape
    sources = source_flux.shape[0]
    rows = observed.shape[0]
    channels = freq_ratio.shape[0]
    times = station_uv.shape[0]
    count = channels * times
    chips = n_dir // 2
    scaling = 1.0 / math.sqrt(sources * n_dir)

    tiles = stations // 128
    gain = station_gain.reshape(count, 2, stations, sources)
    obs = observed.reshape(rows, count, 2, tiles, 128)
    obs = jnp.transpose(obs, (0, 1, 3, 2, 4)).reshape(rows * count * tiles * 2, 128)
    flag_rows = jnp.transpose(flags.reshape(rows, times, tiles, 128), (0, 2, 1, 3))
    flag_rows = flag_rows.reshape(rows * tiles * times, 128)

    vmem = pl.BlockSpec(memory_space=pltpu.VMEM)
    hbm = pl.BlockSpec(memory_space=pl.ANY)
    dma = pltpu.SemaphoreType.DMA
    residual, updated = pl.pallas_call(
        functools.partial(kernel, n_dir, n_freq, scaling),
        out_shape=(
            jax.ShapeDtypeStruct((rows * count * tiles * 2, 128), f32),
            jax.ShapeDtypeStruct((local_dirs, stations), f32),
        ),
        in_specs=[
            pl.BlockSpec(memory_space=pltpu.SMEM),
            hbm,
            vmem,
            vmem,
            vmem,
            vmem,
            hbm,
            hbm,
            vmem,
            hbm,
        ],
        out_specs=(vmem, vmem),
        scratch_shapes=[
            pltpu.VMEM((count, 2, stations, sources), bf16),
            pltpu.VMEM((rows * count * tiles * 2, 128), f32),
            pltpu.VMEM((rows * tiles * times, 128), jnp.int32),
            pltpu.VMEM((stations, stations), f32),
            pltpu.VMEM((count, stations, 8), f32),
            pltpu.VMEM((count, rows, stations), f32),
            pltpu.VMEM((count, stations, 2 * sources), bf16),
            pltpu.VMEM((count, stations, 2 * sources), bf16),
            pltpu.VMEM((count, chips, 2, rows, stations), f32),
            pltpu.VMEM((count, local_dirs, stations, stations), f32),
            pltpu.VMEM((count, chips, rows, stations), bf16),
            pltpu.VMEM((count, chips, rows, stations), bf16),
            pltpu.VMEM((count, chips, rows, stations), bf16),
            pltpu.VMEM((count, 2, rows, stations), f32),
            pltpu.VMEM((count, chips, rows, stations), bf16),
            pltpu.VMEM((count, stations, stations), bf16),
            pltpu.VMEM((local_dirs, stations, 128), f32),
            pltpu.VMEM((local_dirs, 8, stations), f32),
            pltpu.VMEM((n_freq, 8, stations), f32),
            pltpu.VMEM((n_dir, 8, 128), f32),
            pltpu.VMEM((count, tiles, 128, 128), f32),
            dma((count,)),
            dma((3,)),
            dma((count,)),
            dma((count,)),
            dma((count, chips)),
            dma((count, chips)),
            dma((count, chips)),
            dma((count, 2 * chips)),
            dma((count, chips)),
            dma((n_freq,)),
            dma((n_freq,)),
            dma((n_dir,)),
            dma((n_dir,)),
        ],
        compiler_params=pltpu.CompilerParams(
            collective_id=0, has_side_effects=True, vmem_limit_bytes=60 * 1024 * 1024
        ),
        name="calibrate",
    )(
        freq_ratio[None],
        gain,
        station_uv,
        source_lm,
        source_flux,
        source_direction,
        obs,
        flag_rows,
        screen,
        screen_kernel,
    )
    residual = residual.reshape(rows, count, tiles, 2, 128)
    residual = jnp.transpose(residual, (0, 1, 3, 2, 4))
    return (residual.reshape(observed.shape), updated)


def solution(mesh):
    placed = (
        P("dir", "freq", None, None, None),
        P("dir", None, None),
        P("dir", None),
        P(),
        P(),
        P(None, "dir"),
        P("dir"),
        P("freq", None, None, None, "dir"),
        P("dir"),
        P("freq"),
    )
    return jax.shard_map(
        body,
        mesh=mesh,
        in_specs=placed,
        out_specs=(P("dir", "freq", None, None, None), P("dir", None)),
        check_vma=False,
    )
```

```python
import functools
import math

import jax
import jax.numpy as jnp
from jax import lax
from jax.experimental import pallas as pl
from jax.experimental.pallas import tpu as pltpu
from jax.sharding import PartitionSpec as P

step_size = 0.3
epsilon = 1e-06
MESH = pl.DeviceIdType.MESH
f32 = jnp.float32
bf16 = jnp.bfloat16

SIN_POLY = (6.283182818548967, -41.34142139850843, 81.59618386869336, -76.58010048367296, 41.20539468675213, -12.27126208031411)
COS_POLY = (0.9999992215699194, -19.738982515967884, 64.92872660466796, -85.27239684712507, 58.79403796941139, -21.076780928848983)


def horner(coefs, z):
    total = jnp.full_like(z, coefs[-1])
    for c in coefs[-2::-1]:
        total = total * z + c
    return total


def kernel(
    n_dir,
    n_freq,
    scaling,
    ratio_ref,
    gain_hbm,
    uv_ref,
    lm_ref,
    flux_ref,
    dirs_ref,
    obs_hbm,
    flags_hbm,
    screen_ref,
    kern_hbm,
    resid_ref,
    updated_ref,
    gain,
    obs,
    flags,
    kern,
    cols,
    own_res,
    left,
    mixed,
    pfull,
    pdir,
    s1buf,
    r1buf,
    s2buf,
    qown,
    r2buf,
    ugath,
    rowacc,
    colacc,
    gbuf,
    sqbuf,
    tbuf,
    gain_sem,
    in_sem,
    s1_send,
    s1_recv,
    s2_send,
    s2_recv,
    ag_send,
    ag_recv,
    fw_send,
    fr_send,
    fr_recv,
    sq_send,
    sq_recv,
):
    count, _, stations, sources = gain.shape
    local_dirs = pdir.shape[1]
    times = uv_ref.shape[0]
    rows = own_res.shape[1]
    tiles = stations // 128
    chips = n_dir // 2
    me = lax.axis_index("dir")
    fme = lax.axis_index("freq")
    core = lax.rem(me, 2)
    chip = lax.div(me, 2)
    partner = chip * 2 + 1 - core

    def gain_copy(m):
        return pltpu.make_async_copy(gain_hbm.at[m], gain.at[m], gain_sem.at[m])

    for m in range(count):
        gain_copy(m).start()
    in_copies = [
        pltpu.make_async_copy(obs_hbm, obs, in_sem.at[0]),
        pltpu.make_async_copy(flags_hbm, flags, in_sem.at[1]),
        pltpu.make_async_copy(kern_hbm, kern, in_sem.at[2]),
    ]
    for c in in_copies:
        c.start()

    barrier = pltpu.get_barrier_semaphore()
    for o in range(1, n_dir):
        pl.semaphore_signal(
            barrier, inc=1, device_id={"dir": lax.rem(me + o, n_dir)}, device_id_type=MESH
        )
    for o in range(1, n_freq):
        pl.semaphore_signal(
            barrier, inc=1, device_id={"freq": lax.rem(fme + o, n_freq)}, device_id_type=MESH
        )

    for m in range(count):
        ratio = ratio_ref[0, m // times]
        parts = [uv_ref[m % times] * ratio, screen_ref[...] / (ratio * (2.0 * math.pi))]
        parts.append(jnp.zeros((8 - 2 - local_dirs, stations), f32))
        cols[m] = jnp.transpose(jnp.concatenate(parts, axis=0))
    rowacc[...] = jnp.zeros_like(rowacc)
    colacc[...] = jnp.zeros_like(colacc)

    def remote(src, dst, send, recv, axis, where):
        return pltpu.make_async_remote_copy(
            src_ref=src,
            dst_ref=dst,
            send_sem=send,
            recv_sem=recv,
            device_id={axis: where},
            device_id_type=MESH,
        )

    def s1_copy(m):
        return remote(s1buf.at[m], r1buf.at[m], s1_send.at[m], s1_recv.at[m], "dir", partner)

    def s2_copy(m, o):
        to = lax.rem(chip + o, chips)
        return remote(
            s2buf.at[m, to],
            r2buf.at[m, o],
            s2_send.at[m, o],
            s2_recv.at[m, o],
            "dir",
            to * 2 + core,
        )

    def row_slice(owner):
        return pl.ds(pl.multiple_of(owner * rows, rows), rows)

    def ag_copy(m, o):
        to = partner if o == 0 else lax.rem(chip + o, chips) * 2 + core
        piece = ugath.at[m, row_slice(me), :]
        return remote(piece, piece, ag_send.at[m, o], ag_recv.at[m, o], "dir", to)

    def fw_copy(m, o):
        owner = lax.rem(chip - o + chips, chips) * 2 + core
        piece = ugath.at[m, row_slice(owner), :]
        return remote(piece, piece, fw_send.at[m, o], ag_recv.at[m, chips + o - 1], "dir", partner)

    chunk = 32

    def phasors(m):
        gain_copy(m).wait()

        def one(i, _):
            at = pl.ds(pl.multiple_of(i * chunk, chunk), chunk)
            col = cols[m, at, :]
            lm = lm_ref[...]
            turns = col[:, 0:1] * lm[0:1] + col[:, 1:2] * lm[1:2]
            own = jnp.broadcast_to(col[:, 2:3], turns.shape)
            for d in range(1, local_dirs):
                own = jnp.where(dirs_ref[...][None] == d, col[:, 2 + d : 3 + d], own)
            turns = turns + own
            r = turns - jnp.round(turns)
            z = r * r
            amp = jnp.sqrt(flux_ref[...])[None]
            sine = horner(SIN_POLY, z) * (r * amp)
            cosine = horner(COS_POLY, z) * amp
            g_re = gain[m, 0, at, :].astype(f32)
            g_im = gain[m, 1, at, :].astype(f32)
            re = (g_re * cosine - g_im * sine).astype(bf16)
            im = (g_re * sine + g_im * cosine).astype(bf16)
            left[m, at, :sources] = re
            left[m, at, sources:] = im
            mixed[m, at, :sources] = re + im
            mixed[m, at, sources:] = im - re
            return 0

        lax.fori_loop(0, stations // chunk, one, 0)

    def nt_dot(a, b):
        return lax.dot_general(a, b, (((1,), (1,)), ((), ())), preferred_element_type=f32)

    def partial_model(m):
        pfull[m] = nt_dot(mixed[m], left[m]).reshape(chips, 2, rows, stations)

        def one(j, _):
            s1buf[m, j] = pfull[m, j, 1 - core].astype(bf16)
            return 0

        lax.fori_loop(0, chips, one, 0)

    def chip_sum(m):
        s1_copy(m).wait_recv()

        def one(j, _):
            total = pfull[m, j, core] + r1buf[m, j].astype(f32)
            s2buf[m, j] = total.astype(bf16)
            return 0

        lax.fori_loop(0, chips, one, 0)
        for o in range(1, chips):
            s2_copy(m, o).start()
        qown[m] = pfull[m, chip, core] + r1buf[m, chip].astype(f32)

    def own_residual(m):
        total = qown[m]
        for o in range(1, chips):
            s2_copy(m, o).wait_recv()
            total = total + r2buf[m, o].astype(f32)
        row_ids = me * rows + lax.broadcasted_iota(jnp.int32, (rows, 128), 0)
        lane_ids = lax.broadcasted_iota(jnp.int32, (rows, 128), 1)
        for b in range(tiles):
            lanes = slice(b * 128, (b + 1) * 128)
            at = (m * tiles + b) * 2
            real = obs[pl.ds(at, rows, stride=count * tiles * 2), :]
            imag = obs[pl.ds(at + 1, rows, stride=count * tiles * 2), :]
            flag = flags[pl.ds(b * times + lax.rem(m, times), rows, stride=tiles * times), :]
            keep = jnp.where(row_ids == lane_ids + b * 128, 0, flag).astype(f32)
            value = keep * (real + imag - total[:, lanes] * scaling)
            own_res[m, :, lanes] = value
            ugath[m, row_slice(me), lanes] = value.astype(bf16)
        for o in list(range(1, chips)) + [0]:
            ag_copy(m, o).start()

    def forward(m):
        for o in range(1, chips):
            ag_copy(m, o).wait_recv()
            fw_copy(m, o).start()

    def direction_models(m):
        for d in range(local_dirs):
            mask = jnp.where(dirs_ref[...][None] == d, 1.0, 0.0).astype(bf16)
            mask = jnp.concatenate([mask, mask], axis=1)
            pdir[m, d] = nt_dot(left[m] * mask, mixed[m])

    def local_grad(m):
        ag_copy(m, 0).wait_recv()
        for o in range(1, chips):
            fw_copy(m, o).wait_recv()
        weight = scaling / ratio_ref[0, lax.div(m, times)]

        def one(i, carry):
            at = pl.ds(pl.multiple_of(i * chunk, chunk), chunk)
            u = ugath[m, at, :].astype(f32) * weight
            out = []
            for d in range(local_dirs):
                w = u * pdir[m, d, at, :]
                part = w[:, 0:128]
                for b in range(1, stations // 128):
                    part = part + w[:, b * 128 : (b + 1) * 128]
                rowacc[d, at, :] += part
                c = carry[d]
                for b in range(chunk // 8):
                    c = c + w[b * 8 : (b + 1) * 8]
                out.append(c)
            return tuple(out)

        init = tuple(colacc[d] for d in range(local_dirs))
        out = lax.fori_loop(0, stations // chunk, one, init)
        for d in range(local_dirs):
            colacc[d] = out[d]

    group = 128 // rows
    lane0 = pl.multiple_of(lax.div(me, group) * 128, 128)
    sub0 = pl.multiple_of(lax.rem(me, group) * rows, rows)

    def mirror(m):
        for b in range(tiles):
            block = ugath[m, b * 128 : (b + 1) * 128, pl.ds(lane0, 128)].astype(f32)
            tbuf[m, b] = jnp.transpose(block)
        for b in range(tiles):
            turned = tbuf[m, b, pl.ds(sub0, rows), :]
            own = own_res[m, :, b * 128 : (b + 1) * 128]
            at = (m * tiles + b) * 2
            resid_ref[pl.ds(at, rows, stride=count * tiles * 2), :] = (own + turned) * 0.5
            resid_ref[pl.ds(at + 1, rows, stride=count * tiles * 2), :] = (own - turned) * 0.5

    lag = min(3, count - 1)

    def build(s, _):
        phasors(s)
        partial_model(s)

        @pl.when(s == 0)
        def _():
            pl.semaphore_wait(barrier, n_dir - 1 + n_freq - 1)
            for c in in_copies:
                c.wait()

        s1_copy(s).start()

        @pl.when(s >= 1)
        def _():
            chip_sum(s - 1)

        @pl.when(s >= lag)
        def _():
            own_residual(s - lag)

        return 0

    lax.fori_loop(0, count, build, 0)
    chip_sum(count - 1)

    def spread(j, _):
        @pl.when(j < lag)
        def _():
            own_residual(j + count - lag)

        @pl.when(jnp.logical_and(j >= 1, j < count + 1))
        def _():
            forward(j - 1)

        @pl.when(j < count)
        def _():
            direction_models(j)

        @pl.when(j >= 2)
        def _():
            local_grad(j - 2)

            @pl.when(j < count + 1)
            def _():
                mirror(j - 2)

        return 0

    lax.fori_loop(0, count + 2, spread, 0)

    mine = []
    for d in range(local_dirs):
        by_col = jnp.sum(colacc[d], axis=0, keepdims=True)
        by_row = jnp.sum(jnp.transpose(rowacc[d]), axis=0, keepdims=True)
        mine.append(by_col - by_row)
    mine.append(jnp.zeros((8 - local_dirs, stations), f32))
    gbuf[fme] = jnp.concatenate(mine, axis=0)

    def fr_copy(o):
        slot = gbuf.at[fme]
        return remote(
            slot, slot, fr_send.at[o], fr_recv.at[o], "freq", lax.rem(fme + o, n_freq)
        )

    for o in range(1, n_freq):
        fr_copy(o).start()

    mirror(count - 1)

    for o in range(1, n_freq):
        fr_copy(o).wait_recv()
    total = gbuf[0]
    for f in range(1, n_freq):
        total = total + gbuf[f]
    smooth = jnp.dot(
        total, kern[...], preferred_element_type=f32, precision=lax.Precision.HIGHEST
    )
    squares = smooth * smooth
    part = squares[:, 0:128]
    for b in range(1, stations // 128):
        part = part + squares[:, b * 128 : (b + 1) * 128]
    sqbuf[0] = part

    def sq_copy(o):
        return remote(
            sqbuf.at[0], sqbuf.at[o], sq_send.at[o], sq_recv.at[o], "dir", lax.rem(me + o, n_dir)
        )

    for o in range(1, n_dir):
        sq_copy(o).start()
    for o in range(1, n_dir):
        sq_copy(o).wait_recv()
        part = part + sqbuf[o]
    total_sq = jnp.sum(jnp.sum(part, axis=1, keepdims=True), axis=0, keepdims=True)
    scale = step_size * lax.rsqrt(total_sq / (local_dirs * n_dir * stations) + epsilon)
    updated_ref[...] = screen_ref[...] - smooth[:local_dirs] * scale

    def drain(m, _):
        s1_copy(m).wait_send()
        for o in range(1, chips):
            s2_copy(m, o).wait_send()
            fw_copy(m, o).wait_send()
        for o in range(chips):
            ag_copy(m, o).wait_send()
        return 0

    lax.fori_loop(0, count, drain, 0)
    for o in range(1, n_freq):
        fr_copy(o).wait_send()
    for o in range(1, n_dir):
        sq_copy(o).wait_send()


def body(
    observed,
    flags,
    screen,
    screen_kernel,
    station_uv,
    source_lm,
    source_flux,
    station_gain,
    source_direction,
    freq_ratio,
):
    n_dir = lax.axis_size("dir")
    n_freq = lax.axis_size("freq")
    local_dirs, stations = screen.shape
    sources = source_flux.shape[0]
    rows = observed.shape[0]
    channels = freq_ratio.shape[0]
    times = station_uv.shape[0]
    count = channels * times
    chips = n_dir // 2
    scaling = 1.0 / math.sqrt(sources * n_dir)

    tiles = stations // 128
    gain = station_gain.reshape(count, 2, stations, sources)
    obs = observed.reshape(rows, count, 2, tiles, 128)
    obs = jnp.transpose(obs, (0, 1, 3, 2, 4)).reshape(rows * count * tiles * 2, 128)
    flag_rows = jnp.transpose(flags.reshape(rows, times, tiles, 128), (0, 2, 1, 3))
    flag_rows = flag_rows.reshape(rows * tiles * times, 128)

    vmem = pl.BlockSpec(memory_space=pltpu.VMEM)
    hbm = pl.BlockSpec(memory_space=pl.ANY)
    dma = pltpu.SemaphoreType.DMA
    residual, updated = pl.pallas_call(
        functools.partial(kernel, n_dir, n_freq, scaling),
        out_shape=(
            jax.ShapeDtypeStruct((rows * count * tiles * 2, 128), f32),
            jax.ShapeDtypeStruct((local_dirs, stations), f32),
        ),
        in_specs=[
            pl.BlockSpec(memory_space=pltpu.SMEM),
            hbm,
            vmem,
            vmem,
            vmem,
            vmem,
            hbm,
            hbm,
            vmem,
            hbm,
        ],
        out_specs=(vmem, vmem),
        scratch_shapes=[
            pltpu.VMEM((count, 2, stations, sources), bf16),
            pltpu.VMEM((rows * count * tiles * 2, 128), f32),
            pltpu.VMEM((rows * tiles * times, 128), jnp.int32),
            pltpu.VMEM((stations, stations), f32),
            pltpu.VMEM((count, stations, 8), f32),
            pltpu.VMEM((count, rows, stations), f32),
            pltpu.VMEM((count, stations, 2 * sources), bf16),
            pltpu.VMEM((count, stations, 2 * sources), bf16),
            pltpu.VMEM((count, chips, 2, rows, stations), f32),
            pltpu.VMEM((count, local_dirs, stations, stations), f32),
            pltpu.VMEM((count, chips, rows, stations), bf16),
            pltpu.VMEM((count, chips, rows, stations), bf16),
            pltpu.VMEM((count, chips, rows, stations), bf16),
            pltpu.VMEM((count, rows, stations), f32),
            pltpu.VMEM((count, chips, rows, stations), bf16),
            pltpu.VMEM((count, stations, stations), bf16),
            pltpu.VMEM((local_dirs, stations, 128), f32),
            pltpu.VMEM((local_dirs, 8, stations), f32),
            pltpu.VMEM((n_freq, 8, stations), f32),
            pltpu.VMEM((n_dir, 8, 128), f32),
            pltpu.VMEM((count, tiles, 128, 128), f32),
            dma((count,)),
            dma((3,)),
            dma((count,)),
            dma((count,)),
            dma((count, chips)),
            dma((count, chips)),
            dma((count, chips)),
            dma((count, 2 * chips)),
            dma((count, chips)),
            dma((n_freq,)),
            dma((n_freq,)),
            dma((n_dir,)),
            dma((n_dir,)),
        ],
        compiler_params=pltpu.CompilerParams(
            collective_id=0, has_side_effects=True, vmem_limit_bytes=60 * 1024 * 1024
        ),
        name="calibrate",
    )(
        freq_ratio[None],
        gain,
        station_uv,
        source_lm,
        source_flux,
        source_direction,
        obs,
        flag_rows,
        screen,
        screen_kernel,
    )
    residual = residual.reshape(rows, count, tiles, 2, 128)
    residual = jnp.transpose(residual, (0, 1, 3, 2, 4))
    return (residual.reshape(observed.shape), updated)


def solution(mesh):
    placed = (
        P("dir", "freq", None, None, None),
        P("dir", None, None),
        P("dir", None),
        P(),
        P(),
        P(None, "dir"),
        P("dir"),
        P("freq", None, None, None, "dir"),
        P("dir"),
        P("freq"),
    )
    return jax.shard_map(
        body,
        mesh=mesh,
        in_specs=placed,
        out_specs=(P("dir", "freq", None, None, None), P("dir", None)),
        check_vma=False,
    )
```

```python
import functools
import math

import jax
import jax.numpy as jnp
from jax import lax
from jax.experimental import pallas as pl
from jax.experimental.pallas import tpu as pltpu
from jax.sharding import PartitionSpec as P

step_size = 0.3
epsilon = 1e-06
MESH = pl.DeviceIdType.MESH
f32 = jnp.float32
bf16 = jnp.bfloat16

SIN_POLY = (6.283182818548967, -41.34142139850843, 81.59618386869336, -76.58010048367296, 41.20539468675213, -12.27126208031411)
COS_POLY = (0.9999992215699194, -19.738982515967884, 64.92872660466796, -85.27239684712507, 58.79403796941139, -21.076780928848983)


def horner(coefs, z):
    total = jnp.full_like(z, coefs[-1])
    for c in coefs[-2::-1]:
        total = total * z + c
    return total


def kernel(
    n_dir,
    n_freq,
    scaling,
    ratio_ref,
    gain_hbm,
    uv_ref,
    lm_ref,
    flux_ref,
    dirs_ref,
    obs_hbm,
    flags_hbm,
    screen_ref,
    kern_hbm,
    resid_ref,
    updated_ref,
    gain,
    obs,
    flags,
    kern,
    cols,
    own_res,
    left,
    mixed,
    pfull,
    pdir,
    s1buf,
    r1buf,
    s2buf,
    qown,
    r2buf,
    ugath,
    rowacc,
    colacc,
    gbuf,
    sqbuf,
    tbuf,
    gain_sem,
    in_sem,
    s1_send,
    s1_recv,
    s2_send,
    s2_recv,
    ag_send,
    ag_recv,
    fw_send,
    fr_send,
    fr_recv,
    sq_send,
    sq_recv,
):
    count, _, stations, sources = gain.shape
    local_dirs = pdir.shape[1]
    times = uv_ref.shape[0]
    rows = own_res.shape[1]
    tiles = stations // 128
    chips = n_dir // 2
    me = lax.axis_index("dir")
    fme = lax.axis_index("freq")
    core = lax.rem(me, 2)
    chip = lax.div(me, 2)
    partner = chip * 2 + 1 - core

    def gain_copy(m):
        return pltpu.make_async_copy(gain_hbm.at[m], gain.at[m], gain_sem.at[m])

    for m in range(count):
        gain_copy(m).start()
    in_copies = [
        pltpu.make_async_copy(obs_hbm, obs, in_sem.at[0]),
        pltpu.make_async_copy(flags_hbm, flags, in_sem.at[1]),
        pltpu.make_async_copy(kern_hbm, kern, in_sem.at[2]),
    ]
    for c in in_copies:
        c.start()

    barrier = pltpu.get_barrier_semaphore()
    for o in range(1, n_dir):
        pl.semaphore_signal(
            barrier, inc=1, device_id={"dir": lax.rem(me + o, n_dir)}, device_id_type=MESH
        )
    for o in range(1, n_freq):
        pl.semaphore_signal(
            barrier, inc=1, device_id={"freq": lax.rem(fme + o, n_freq)}, device_id_type=MESH
        )

    for m in range(count):
        ratio = ratio_ref[0, m // times]
        parts = [uv_ref[m % times] * ratio, screen_ref[...] / (ratio * (2.0 * math.pi))]
        parts.append(jnp.zeros((8 - 2 - local_dirs, stations), f32))
        cols[m] = jnp.transpose(jnp.concatenate(parts, axis=0))
    rowacc[...] = jnp.zeros_like(rowacc)
    colacc[...] = jnp.zeros_like(colacc)

    def remote(src, dst, send, recv, axis, where):
        return pltpu.make_async_remote_copy(
            src_ref=src,
            dst_ref=dst,
            send_sem=send,
            recv_sem=recv,
            device_id={axis: where},
            device_id_type=MESH,
        )

    def s1_copy(m):
        return remote(s1buf.at[m], r1buf.at[m], s1_send.at[m], s1_recv.at[m], "dir", partner)

    def s2_copy(m, o):
        to = lax.rem(chip + o, chips)
        return remote(
            s2buf.at[m, to],
            r2buf.at[m, o],
            s2_send.at[m, o],
            s2_recv.at[m, o],
            "dir",
            to * 2 + core,
        )

    def row_slice(owner):
        return pl.ds(pl.multiple_of(owner * rows, rows), rows)

    def ag_copy(m, o):
        to = partner if o == 0 else lax.rem(chip + o, chips) * 2 + core
        piece = ugath.at[m, row_slice(me), :]
        return remote(piece, piece, ag_send.at[m, o], ag_recv.at[m, o], "dir", to)

    def fw_copy(m, o):
        owner = lax.rem(chip - o + chips, chips) * 2 + core
        piece = ugath.at[m, row_slice(owner), :]
        return remote(piece, piece, fw_send.at[m, o], ag_recv.at[m, chips + o - 1], "dir", partner)

    chunk = 32

    def phasors(m):
        gain_copy(m).wait()

        def one(i, _):
            at = pl.ds(pl.multiple_of(i * chunk, chunk), chunk)
            col = cols[m, at, :]
            lm = lm_ref[...]
            turns = col[:, 0:1] * lm[0:1] + col[:, 1:2] * lm[1:2]
            own = jnp.broadcast_to(col[:, 2:3], turns.shape)
            for d in range(1, local_dirs):
                own = jnp.where(dirs_ref[...][None] == d, col[:, 2 + d : 3 + d], own)
            turns = turns + own
            r = turns - jnp.round(turns)
            z = r * r
            amp = jnp.sqrt(flux_ref[...])[None]
            sine = horner(SIN_POLY, z) * (r * amp)
            cosine = horner(COS_POLY, z) * amp
            g_re = gain[m, 0, at, :].astype(f32)
            g_im = gain[m, 1, at, :].astype(f32)
            re = (g_re * cosine - g_im * sine).astype(bf16)
            im = (g_re * sine + g_im * cosine).astype(bf16)
            left[m, at, :sources] = re
            left[m, at, sources:] = im
            mixed[m, at, :sources] = re + im
            mixed[m, at, sources:] = im - re
            return 0

        lax.fori_loop(0, stations // chunk, one, 0)

    def nt_dot(a, b):
        return lax.dot_general(a, b, (((1,), (1,)), ((), ())), preferred_element_type=f32)

    def partial_model(m):
        pfull[m] = nt_dot(mixed[m], left[m]).reshape(chips, 2, rows, stations)

        def one(j, _):
            s1buf[m, j] = pfull[m, j, 1 - core].astype(bf16)
            return 0

        lax.fori_loop(0, chips, one, 0)

    def chip_sum(m):
        s1_copy(m).wait_recv()

        def one(j, _):
            total = pfull[m, j, core] + r1buf[m, j].astype(f32)
            s2buf[m, j] = total.astype(bf16)
            return 0

        lax.fori_loop(0, chips, one, 0)
        for o in range(1, chips):
            s2_copy(m, o).start()
        qown[m] = pfull[m, chip, core] + r1buf[m, chip].astype(f32)

    def own_residual(m):
        total = qown[m]
        for o in range(1, chips):
            s2_copy(m, o).wait_recv()
            total = total + r2buf[m, o].astype(f32)
        row_ids = me * rows + lax.broadcasted_iota(jnp.int32, (rows, 128), 0)
        lane_ids = lax.broadcasted_iota(jnp.int32, (rows, 128), 1)
        for b in range(tiles):
            lanes = slice(b * 128, (b + 1) * 128)
            at = (m * tiles + b) * 2
            real = obs[pl.ds(at, rows, stride=count * tiles * 2), :]
            imag = obs[pl.ds(at + 1, rows, stride=count * tiles * 2), :]
            flag = flags[pl.ds(b * times + lax.rem(m, times), rows, stride=tiles * times), :]
            keep = jnp.where(row_ids == lane_ids + b * 128, 0, flag).astype(f32)
            value = keep * (real + imag - total[:, lanes] * scaling)
            own_res[m, :, lanes] = value
            ugath[m, row_slice(me), lanes] = value.astype(bf16)
        for o in list(range(1, chips)) + [0]:
            ag_copy(m, o).start()

    def forward(m):
        for o in range(1, chips):
            ag_copy(m, o).wait_recv()
            fw_copy(m, o).start()

    def direction_models(m):
        for d in range(local_dirs):
            mask = jnp.where(dirs_ref[...][None] == d, 1.0, 0.0).astype(bf16)
            mask = jnp.concatenate([mask, mask], axis=1)
            pdir[m, d] = nt_dot(left[m] * mask, mixed[m])

    def local_grad(m):
        ag_copy(m, 0).wait_recv()
        for o in range(1, chips):
            fw_copy(m, o).wait_recv()
        weight = scaling / ratio_ref[0, lax.div(m, times)]

        def one(i, carry):
            at = pl.ds(pl.multiple_of(i * chunk, chunk), chunk)
            u = ugath[m, at, :].astype(f32) * weight
            out = []
            for d in range(local_dirs):
                w = u * pdir[m, d, at, :]
                part = w[:, 0:128]
                for b in range(1, stations // 128):
                    part = part + w[:, b * 128 : (b + 1) * 128]
                rowacc[d, at, :] += part
                c = carry[d]
                for b in range(chunk // 8):
                    c = c + w[b * 8 : (b + 1) * 8]
                out.append(c)
            return tuple(out)

        init = tuple(colacc[d] for d in range(local_dirs))
        out = lax.fori_loop(0, stations // chunk, one, init)
        for d in range(local_dirs):
            colacc[d] = out[d]

    group = 128 // rows
    lane0 = pl.multiple_of(lax.div(me, group) * 128, 128)
    sub0 = pl.multiple_of(lax.rem(me, group) * rows, rows)

    def mirror(m):
        for b in range(tiles):
            block = ugath[m, b * 128 : (b + 1) * 128, pl.ds(lane0, 128)].astype(f32)
            tbuf[m, b] = jnp.transpose(block)
        for b in range(tiles):
            turned = tbuf[m, b, pl.ds(sub0, rows), :]
            own = own_res[m, :, b * 128 : (b + 1) * 128]
            at = (m * tiles + b) * 2
            resid_ref[pl.ds(at, rows, stride=count * tiles * 2), :] = (own + turned) * 0.5
            resid_ref[pl.ds(at + 1, rows, stride=count * tiles * 2), :] = (own - turned) * 0.5

    lag = min(3, count - 1)

    def build(s, _):
        phasors(s)
        partial_model(s)

        @pl.when(s == 0)
        def _():
            pl.semaphore_wait(barrier, n_dir - 1 + n_freq - 1)
            for c in in_copies:
                c.wait()

        s1_copy(s).start()

        @pl.when(s >= 1)
        def _():
            chip_sum(s - 1)

        @pl.when(s >= lag)
        def _():
            own_residual(s - lag)

        return 0

    lax.fori_loop(0, count, build, 0)
    chip_sum(count - 1)

    def spread(j, _):
        @pl.when(j < lag)
        def _():
            own_residual(j + count - lag)

        @pl.when(jnp.logical_and(j >= 1, j < count + 1))
        def _():
            forward(j - 1)

        @pl.when(j < count)
        def _():
            direction_models(j)

        @pl.when(j >= 2)
        def _():
            local_grad(j - 2)

            @pl.when(j < count + 1)
            def _():
                mirror(j - 2)

        return 0

    lax.fori_loop(0, count + 2, spread, 0)

    mine = []
    for d in range(local_dirs):
        by_col = jnp.sum(colacc[d], axis=0, keepdims=True)
        by_row = jnp.sum(jnp.transpose(rowacc[d]), axis=0, keepdims=True)
        mine.append(by_col - by_row)
    mine.append(jnp.zeros((8 - local_dirs, stations), f32))
    gbuf[fme] = jnp.concatenate(mine, axis=0)

    def fr_copy(o):
        slot = gbuf.at[fme]
        return remote(
            slot, slot, fr_send.at[o], fr_recv.at[o], "freq", lax.rem(fme + o, n_freq)
        )

    for o in range(1, n_freq):
        fr_copy(o).start()

    mirror(count - 1)

    for o in range(1, n_freq):
        fr_copy(o).wait_recv()
    total = gbuf[0]
    for f in range(1, n_freq):
        total = total + gbuf[f]
    smooth = jnp.dot(
        total, kern[...], preferred_element_type=f32, precision=lax.Precision.HIGHEST
    )
    squares = smooth * smooth
    part = squares[:, 0:128]
    for b in range(1, stations // 128):
        part = part + squares[:, b * 128 : (b + 1) * 128]
    sqbuf[0] = part

    def sq_copy(o):
        return remote(
            sqbuf.at[0], sqbuf.at[o], sq_send.at[o], sq_recv.at[o], "dir", lax.rem(me + o, n_dir)
        )

    for o in range(1, n_dir):
        sq_copy(o).start()
    for o in range(1, n_dir):
        sq_copy(o).wait_recv()
        part = part + sqbuf[o]
    total_sq = jnp.sum(jnp.sum(part, axis=1, keepdims=True), axis=0, keepdims=True)
    scale = step_size * lax.rsqrt(total_sq / (local_dirs * n_dir * stations) + epsilon)
    updated_ref[...] = screen_ref[...] - smooth[:local_dirs] * scale

    def drain(m, _):
        s1_copy(m).wait_send()
        for o in range(1, chips):
            s2_copy(m, o).wait_send()
            fw_copy(m, o).wait_send()
        for o in range(chips):
            ag_copy(m, o).wait_send()
        return 0

    lax.fori_loop(0, count, drain, 0)
    for o in range(1, n_freq):
        fr_copy(o).wait_send()
    for o in range(1, n_dir):
        sq_copy(o).wait_send()


def hand_over(resid_ref, updated_ref, resid_out, updated_out):
    resid_out[...] = resid_ref[...]
    updated_out[...] = updated_ref[...]


def body(
    observed,
    flags,
    screen,
    screen_kernel,
    station_uv,
    source_lm,
    source_flux,
    station_gain,
    source_direction,
    freq_ratio,
):
    n_dir = lax.axis_size("dir")
    n_freq = lax.axis_size("freq")
    local_dirs, stations = screen.shape
    sources = source_flux.shape[0]
    rows = observed.shape[0]
    channels = freq_ratio.shape[0]
    times = station_uv.shape[0]
    count = channels * times
    chips = n_dir // 2
    scaling = 1.0 / math.sqrt(sources * n_dir)

    tiles = stations // 128
    gain = station_gain.reshape(count, 2, stations, sources)
    obs = observed.reshape(rows, count, 2, tiles, 128)
    obs = jnp.transpose(obs, (0, 1, 3, 2, 4)).reshape(rows * count * tiles * 2, 128)
    flag_rows = jnp.transpose(flags.reshape(rows, times, tiles, 128), (0, 2, 1, 3))
    flag_rows = flag_rows.reshape(rows * tiles * times, 128)

    vmem = pl.BlockSpec(memory_space=pltpu.VMEM)
    hbm = pl.BlockSpec(memory_space=pl.ANY)
    dma = pltpu.SemaphoreType.DMA
    residual, updated = pl.pallas_call(
        functools.partial(kernel, n_dir, n_freq, scaling),
        out_shape=(
            jax.ShapeDtypeStruct((rows * count * tiles * 2, 128), f32),
            jax.ShapeDtypeStruct((local_dirs, stations), f32),
        ),
        in_specs=[
            pl.BlockSpec(memory_space=pltpu.SMEM),
            hbm,
            vmem,
            vmem,
            vmem,
            vmem,
            hbm,
            hbm,
            vmem,
            hbm,
        ],
        out_specs=(vmem, vmem),
        scratch_shapes=[
            pltpu.VMEM((count, 2, stations, sources), bf16),
            pltpu.VMEM((rows * count * tiles * 2, 128), f32),
            pltpu.VMEM((rows * tiles * times, 128), jnp.int32),
            pltpu.VMEM((stations, stations), f32),
            pltpu.VMEM((count, stations, 8), f32),
            pltpu.VMEM((count, rows, stations), f32),
            pltpu.VMEM((count, stations, 2 * sources), bf16),
            pltpu.VMEM((count, stations, 2 * sources), bf16),
            pltpu.VMEM((count, chips, 2, rows, stations), f32),
            pltpu.VMEM((count, local_dirs, stations, stations), f32),
            pltpu.VMEM((count, chips, rows, stations), bf16),
            pltpu.VMEM((count, chips, rows, stations), bf16),
            pltpu.VMEM((count, chips, rows, stations), bf16),
            pltpu.VMEM((count, rows, stations), f32),
            pltpu.VMEM((count, chips, rows, stations), bf16),
            pltpu.VMEM((count, stations, stations), bf16),
            pltpu.VMEM((local_dirs, stations, 128), f32),
            pltpu.VMEM((local_dirs, 8, stations), f32),
            pltpu.VMEM((n_freq, 8, stations), f32),
            pltpu.VMEM((n_dir, 8, 128), f32),
            pltpu.VMEM((count, tiles, 128, 128), f32),
            dma((count,)),
            dma((3,)),
            dma((count,)),
            dma((count,)),
            dma((count, chips)),
            dma((count, chips)),
            dma((count, chips)),
            dma((count, 2 * chips)),
            dma((count, chips)),
            dma((n_freq,)),
            dma((n_freq,)),
            dma((n_dir,)),
            dma((n_dir,)),
        ],
        compiler_params=pltpu.CompilerParams(
            collective_id=0, has_side_effects=True, vmem_limit_bytes=60 * 1024 * 1024
        ),
        name="calibrate",
    )(
        freq_ratio[None],
        gain,
        station_uv,
        source_lm,
        source_flux,
        source_direction,
        obs,
        flag_rows,
        screen,
        screen_kernel,
    )
    halves = 2
    block = pl.BlockSpec((residual.shape[0] // halves, 128), lambda i: (i, 0))
    small = pl.BlockSpec((local_dirs, stations), lambda i: (0, 0))
    residual, updated = pl.pallas_call(
        hand_over,
        grid=(halves,),
        out_shape=(
            jax.ShapeDtypeStruct(residual.shape, f32),
            jax.ShapeDtypeStruct(updated.shape, f32),
        ),
        in_specs=[block, small],
        out_specs=(block, small),
        name="results",
    )(residual, updated)
    residual = residual.reshape(rows, count, tiles, 2, 128)
    residual = jnp.transpose(residual, (0, 1, 3, 2, 4))
    return (residual.reshape(observed.shape), updated)


def solution(mesh):
    placed = (
        P("dir", "freq", None, None, None),
        P("dir", None, None),
        P("dir", None),
        P(),
        P(),
        P(None, "dir"),
        P("dir"),
        P("freq", None, None, None, "dir"),
        P("dir"),
        P("freq"),
    )
    return jax.shard_map(
        body,
        mesh=mesh,
        in_specs=placed,
        out_specs=(P("dir", "freq", None, None, None), P("dir", None)),
        check_vma=False,
    )
```
